512 devices in a mesh: blk: 128 (over z, y, core), head: 4 (over x).
Axes of the slice: x: 4, y: 8, z: 8, core: 2. Of those that a mesh axis runs over, the one named last changes fastest.
Arguments:
- layer_entry_vectors: bfloat16 [1024, 16, 2048], P('blk', None, 'head'), may hold values from -6 to 6
- guessed_lookup_vectors: bfloat16 [1024, 16, 2048], P('blk', None, 'head'), may hold values from -3 to 3
- guessed_content_vectors: bfloat16 [1024, 16, 2048], P('blk', None, 'head'), may hold values from -6 to 6
- gating_query: bfloat16 [1024, 16, 2048], P('blk', 'head'), may hold values from -6 to 6
- lane_memory_store: float32 [4, 16384, 2048], P('head', 'blk'), may hold values from -3 to 3
- prior_step_store: float32 [4, 16384, 32], P('head', 'blk'), may hold values from -6 to 6
- fading_blend_ratio: float32 [2048], P('head'), may hold values from 0 to 1
- learning_speed_blend: float32 [2048], P('head'), may hold values from 0 to 1
- fading_left_factor: bfloat16 [2048, 96], P('head'), may hold values from -0.125 to 0.125
- fading_right_factor: bfloat16 [96, 2048], P(None, 'head'), may hold values from -0.625 to 0.625
- fading_offset: float32 [2048], P('head'), may hold values from -6 to 1
- learning_speed_left: bfloat16 [2048, 96], P('head'), may hold values from -0.125 to 0.125
- learning_speed_right: bfloat16 [96, 2048], P(None, 'head'), may hold values from -0.625 to 0.625
- learning_speed_offset: float32 [2048], P('head'), may hold values from -2 to 2
- erasing_lookup_factor: float32 [2048], P('head'), may hold values from 0.1 to 1.9
- written_lookup_factor: float32 [2048], P('head'), may hold values from 0 to 1
- present_reward_factors: float32 [2048], P('head'), may hold values from -3 to 3
- lane_standard_factor: float32 [2048], P('head'), may hold values from 0.1 to 1.9
- lane_standard_offset: float32 [2048], P('head'), may hold values from -2 to 2
- caller_memory_directory: int32 [1024, 32, 2], P(None, 'head'), may hold values from 0 to 16383, as said below
- kept_target_place: int32 [1024, 32, 2], P(None, 'head'), may hold values from 0 to 16383, as said below
- caller_sequence: int32 [1024], replicated, may hold values from 0 to 1023, as said below
- approved_guesses: int32 [1024], replicated, may hold values from 0 to 16
Outputs:
- temporal_blend_result: bfloat16 [1024, 16, 2048], P('blk', None, 'head')
- new_states: float32 [4, 16384, 2048], P('head', 'blk')
- new_edges: float32 [4, 16384, 32], P('head', 'blk')
The draws below stay inside these ranges and needn't reach their ends.
Inputs may be any that keep to these rules, and one draw needn't show every extreme that they name: `caller_memory_directory`: every entry names a slot of the pool of head group h // 8; all entries of one head group are distinct and cover its 16384 slots. For the positions p of one blk index, taken through q = caller_sequence[p], exactly 1 of the slots of each head group lie on each blk index (slot // 128). `kept_target_place`: same rules as the page table: every slot of a head group is written exactly once, and one blk index's positions write exactly 1 slots of each head group on each blk index. `caller_sequence`: A permutation of the 1024 requests.
All inputs are finite; a program needn't handle non-finite values.
Results may differ from the reference program's by a relative error of at most 0.006.
Values may be sent and summed in bfloat16 or wider, within the bound.
A program may use at most 64 MiB of HBM per device.

```python
import jax
import jax.numpy as jnp
from jax import lax

EMBEDDING_SIZE = 2048
ATTENTION_LANES = 32
LANE_SIZE = 64
LR_W = 96
LR_A = 96
PROPOSED_STEPS = 16
SLOT_ROWS = 32
HEAD_DEV = 8
HALVES = 2
SLOT_DEV = 128
PEER_SLOTS = 1
CALLER_TOTAL = 1024
SLOTS = 16384
GROUPS = 4
BLOCKS = 128
N_HEAD = 4


def shuffle_rows(row_key):
    return jax.random.permutation(row_key, SLOT_DEV).astype(jnp.int32)


def routed_slots(base_key, stream):
    stream_key = jax.random.fold_in(base_key, stream)
    source = jnp.arange(BLOCKS, dtype=jnp.int32)[:, None]
    columns = []
    for group_index in range(GROUPS):
        group_key = jax.random.fold_in(stream_key, group_index)
        spread = jax.vmap(shuffle_rows)(jax.random.split(jax.random.fold_in(group_key, 1), BLOCKS))
        within = jax.vmap(shuffle_rows)(jax.random.split(jax.random.fold_in(group_key, 2), BLOCKS))
        holder = (source + spread // PEER_SLOTS) % BLOCKS
        arrival = source * PEER_SLOTS + spread % PEER_SLOTS
        slot_ids = holder * SLOT_DEV + within[holder, arrival]
        columns.append(slot_ids.reshape(CALLER_TOTAL, HEAD_DEV, HALVES))
    return jnp.concatenate(columns, axis=1).astype(jnp.int32)


def serving(base_key):
    return jax.random.permutation(jax.random.fold_in(base_key, 5), CALLER_TOTAL).astype(jnp.int32)


def draw_caller_sequence(key, part):
    return serving(key)


def draw_caller_memory_directory(key, part):
    slot_table = routed_slots(key, 11)
    return jnp.zeros_like(slot_table).at[serving(key)].set(slot_table)


def draw_kept_target_place(key, part):
    slot_table = routed_slots(key, 13)
    return jnp.zeros_like(slot_table).at[serving(key)].set(slot_table)


def with_ends(entries, key, low, top_value):
    spot = [jax.random.randint(jax.random.fold_in(key, axis), (), 0, length) for axis, length in enumerate(entries.shape)]
    widest = entries.shape.index(max(entries.shape))
    neighbour = spot[:widest] + [(spot[widest] + 1) % entries.shape[widest]] + spot[widest + 1:]
    return entries.at[tuple(spot)].set(low).at[tuple(neighbour)].set(top_value)


def levels(key, dims, pieces, least, high):
    factor_of, own = 1.0, jax.random.fold_in(key, 6)
    for position, parts in pieces:
        draws = jnp.exp(jax.random.uniform(jax.random.fold_in(own, position), (parts,), jnp.float32, least / len(pieces), high / len(pieces)))
        factor_of = factor_of * jnp.repeat(draws, dims[position] // parts).reshape([-1 if axis == position else 1 for axis in range(len(dims))])
    return factor_of


def scatter_about(own_key, shape, scale, bound, cuts=(), held_as=jnp.bfloat16):
    entries = jax.random.normal(own_key, shape, jnp.float32) * scale
    if len(cuts) > 0:
        entries = levels(own_key, shape, cuts, -0.22, 0.18) * entries
    return jnp.clip(entries, min=-bound, max=bound).astype(held_as)


def setup_inputs(seed: int = 0) -> dict:
    splits = jax.random.split(jax.random.key(seed), 24)
    return {
        "layer_entry_vectors": scatter_about(splits[0], (CALLER_TOTAL, PROPOSED_STEPS, EMBEDDING_SIZE), 1.0, 6.0, ((0, 128), (2, 4))),
        "guessed_lookup_vectors": scatter_about(splits[1], (CALLER_TOTAL, PROPOSED_STEPS, EMBEDDING_SIZE), 0.5, 3.0, ((0, 128), (2, 4))),
        "guessed_content_vectors": scatter_about(splits[2], (CALLER_TOTAL, PROPOSED_STEPS, EMBEDDING_SIZE), 1.0, 6.0, ((0, 128), (2, 4))),
        "gating_query": scatter_about(splits[3], (CALLER_TOTAL, PROPOSED_STEPS, EMBEDDING_SIZE), 1.0, 6.0, ((0, 128), (1, 4))),
        "lane_memory_store": scatter_about(splits[4], (GROUPS, SLOTS, SLOT_ROWS * LANE_SIZE), 0.5, 3.0, ((0, 4), (1, 128)), jnp.float32),
        "prior_step_store": scatter_about(splits[5], (GROUPS, SLOTS, SLOT_ROWS), 1.0, 6.0, ((0, 4), (1, 128)), jnp.float32),
        "fading_blend_ratio": jnp.clip(1.0 * jax.random.uniform(splits[6], (EMBEDDING_SIZE,), jnp.float32) ** levels(splits[6], (EMBEDDING_SIZE,), ((0, 4),), -0.2, 0.2), 0.0, 1.0),
        "learning_speed_blend": jnp.clip(1.0 * jax.random.uniform(splits[7], (EMBEDDING_SIZE,), jnp.float32) ** levels(splits[7], (EMBEDDING_SIZE,), ((0, 4),), -0.2, 0.2), 0.0, 1.0),
        "fading_left_factor": scatter_about(splits[8], (EMBEDDING_SIZE, LR_W), EMBEDDING_SIZE ** -0.5, 0.125, ((0, 4),)),
        "fading_right_factor": scatter_about(splits[9], (LR_W, EMBEDDING_SIZE), LR_W ** -0.5, 0.625, ((1, 4),)),
        "fading_offset": jnp.clip(-6.0 + 7.0 * jax.random.uniform(splits[10], (EMBEDDING_SIZE,), jnp.float32) ** levels(splits[10], (EMBEDDING_SIZE,), ((0, 4),), -0.2, 0.2), -6.0, 1.0),
        "learning_speed_left": scatter_about(splits[11], (EMBEDDING_SIZE, LR_A), EMBEDDING_SIZE ** -0.5, 0.125, ((0, 4),)),
        "learning_speed_right": scatter_about(splits[12], (LR_A, EMBEDDING_SIZE), LR_A ** -0.5, 0.625, ((1, 4),)),
        "learning_speed_offset": jnp.clip(jax.random.uniform(splits[13], (EMBEDDING_SIZE,), jnp.float32, -2.0, 2.0) * levels(splits[13], (EMBEDDING_SIZE,), ((0, 4),), -0.4, 0.0), -2.0, 2.0),
        "erasing_lookup_factor": jnp.clip(1.0 + 0.18 * jax.random.normal(splits[14], (EMBEDDING_SIZE,), jnp.float32), 0.1, 1.9),
        "written_lookup_factor": jnp.clip(1.0 * jax.random.uniform(splits[15], (EMBEDDING_SIZE,), jnp.float32) ** levels(splits[15], (EMBEDDING_SIZE,), ((0, 4),), -0.2, 0.2), 0.0, 1.0),
        "present_reward_factors": scatter_about(splits[16], (EMBEDDING_SIZE,), 0.5, 3.0, ((0, 4),), jnp.float32),
        "lane_standard_factor": jnp.clip(1.0 + 0.18 * jax.random.normal(splits[17], (EMBEDDING_SIZE,), jnp.float32), 0.1, 1.9),
        "lane_standard_offset": scatter_about(splits[18], (EMBEDDING_SIZE,), 0.3, 2.0, ((0, 4),), jnp.float32),
        "caller_memory_directory": draw_caller_memory_directory(jax.random.fold_in(splits[23], 71), 0),
        "kept_target_place": draw_kept_target_place(jax.random.fold_in(splits[23], 71), 0),
        "caller_sequence": draw_caller_sequence(jax.random.fold_in(splits[23], 71), 0),
        "approved_guesses": with_ends(jax.random.randint(splits[22], (CALLER_TOTAL,), 0, PROPOSED_STEPS + 1), jax.random.fold_in(splits[22], 1), 0, PROPOSED_STEPS).astype(jnp.int32),
    }


EPSILON = 1e-05
NORM_EPSILON = 0.00064

def head_scan(packed, counts):
    start_state, forget, unit_key, in_rate, adjusted_lookup, content_lines, gating_query_lines = packed

    def advance(carried, per_step):
        carry_state, accepted_state = carried
        step_index, forget_t, unit_t, rate_t, key_t, value_t, recept_t = per_step
        projected = lax.optimization_barrier(jnp.sum(carry_state * unit_t[:, None, :], axis=-1))
        carry_state = carry_state * forget_t[:, None, :] - projected[:, :, None] * (rate_t * unit_t)[:, None, :] + value_t[:, :, None] * key_t[:, None, :]
        output = lax.optimization_barrier(jnp.sum(carry_state * recept_t[:, None, :], axis=-1))
        accepted_state = jnp.where((counts == step_index + 1)[:, None, None], carry_state, accepted_state)
        return ((carry_state, accepted_state), output)
    step_ids = jnp.arange(PROPOSED_STEPS, dtype=jnp.int32)
    carried, outputs = lax.scan(advance, (start_state, start_state), (step_ids, forget, unit_key, in_rate, adjusted_lookup, content_lines, gating_query_lines))
    return (outputs, carried[1])

def reference(layer_entry_vectors, guessed_lookup_vectors, guessed_content_vectors, gating_query, lane_memory_store, prior_step_store, fading_blend_ratio, learning_speed_blend, fading_left_factor, fading_right_factor, fading_offset, learning_speed_left, learning_speed_right, learning_speed_offset, erasing_lookup_factor, written_lookup_factor, present_reward_factors, lane_standard_factor, lane_standard_offset, caller_memory_directory, kept_target_place, caller_sequence, approved_guesses):
    heads_on_device = ATTENTION_LANES // N_HEAD
    halves = LANE_SIZE // SLOT_ROWS
    group_ids = (jnp.arange(ATTENTION_LANES, dtype=jnp.int32) // heads_on_device)[None, :, None]
    counts = approved_guesses[caller_sequence]
    wanted = caller_memory_directory[caller_sequence]
    targets = kept_target_place[caller_sequence]
    start_states = lane_memory_store[group_ids, wanted].reshape(CALLER_TOTAL, ATTENTION_LANES, LANE_SIZE, LANE_SIZE)
    edge_rows = prior_step_store[group_ids, wanted].reshape(CALLER_TOTAL, EMBEDDING_SIZE)
    current = layer_entry_vectors.astype(jnp.float32)
    previous = jnp.concatenate([edge_rows[:, None, :], current[:, :-1]], axis=1)
    shift_delta = previous - current
    row_count = CALLER_TOTAL * PROPOSED_STEPS
    mixed_decay = (current + shift_delta * fading_blend_ratio).astype(jnp.bfloat16).reshape(row_count, EMBEDDING_SIZE)
    mixed_rate = (current + shift_delta * learning_speed_blend).astype(jnp.bfloat16).reshape(row_count, EMBEDDING_SIZE)
    decay_inner = jnp.tanh(jnp.dot(mixed_decay, fading_left_factor, preferred_element_type=jnp.float32)).astype(jnp.bfloat16)
    rate_inner = jnp.dot(mixed_rate, learning_speed_left, preferred_element_type=jnp.float32).astype(jnp.bfloat16)
    decay_term = jnp.dot(decay_inner, fading_right_factor, preferred_element_type=jnp.float32).reshape(CALLER_TOTAL, PROPOSED_STEPS, EMBEDDING_SIZE)
    rate_term = jnp.dot(rate_inner, learning_speed_right, preferred_element_type=jnp.float32).reshape(CALLER_TOTAL, PROPOSED_STEPS, EMBEDDING_SIZE)
    log_forget = -jax.nn.softplus(-(fading_offset + decay_term)) - 0.5
    forget = jnp.exp(-jnp.exp(log_forget))
    in_rate = jax.nn.sigmoid(learning_speed_offset + rate_term)
    key_full = guessed_lookup_vectors.astype(jnp.float32)
    grouped = (key_full * erasing_lookup_factor).reshape(CALLER_TOTAL, PROPOSED_STEPS, ATTENTION_LANES, LANE_SIZE)
    unit_key = grouped * lax.rsqrt(lax.optimization_barrier(jnp.sum(grouped * grouped, axis=-1, keepdims=True)) + EPSILON)
    adjusted_lookup = key_full * (1.0 + (in_rate - 1.0) * written_lookup_factor)
    content_lines = guessed_content_vectors.astype(jnp.float32)
    gating_query_lines = gating_query.astype(jnp.float32)

    def by_head(array):
        return jnp.transpose(array.reshape(CALLER_TOTAL, PROPOSED_STEPS, ATTENTION_LANES, LANE_SIZE), (2, 1, 0, 3))

    def run_head(packed):
        return head_scan(packed, counts)
    outputs, accepted_states = lax.map(run_head, (jnp.transpose(start_states, (1, 0, 2, 3)), by_head(forget), by_head(unit_key), by_head(in_rate), by_head(adjusted_lookup), by_head(content_lines), by_head(gating_query_lines)))
    outputs = jnp.transpose(outputs, (2, 1, 0, 3))
    average = lax.optimization_barrier(jnp.mean(outputs, axis=-1, keepdims=True))
    centered = outputs - average
    variance = lax.optimization_barrier(jnp.mean(centered * centered, axis=-1, keepdims=True))
    standardized_lines = centered * lax.rsqrt(variance + NORM_EPSILON) * lane_standard_factor.reshape(ATTENTION_LANES, LANE_SIZE) + lane_standard_offset.reshape(ATTENTION_LANES, LANE_SIZE)
    present_reward_term = lax.optimization_barrier(jnp.sum((gating_query_lines * adjusted_lookup * present_reward_factors).reshape(CALLER_TOTAL, PROPOSED_STEPS, ATTENTION_LANES, LANE_SIZE), axis=-1, keepdims=True)) * content_lines.reshape(CALLER_TOTAL, PROPOSED_STEPS, ATTENTION_LANES, LANE_SIZE)
    temporal_blend_result = (standardized_lines + present_reward_term).astype(jnp.bfloat16).reshape(CALLER_TOTAL, PROPOSED_STEPS, EMBEDDING_SIZE)
    last_token = jnp.maximum(counts - 1, 0).astype(jnp.int32)
    picked = jnp.take_along_axis(current, last_token[:, None, None], axis=1)[:, 0]
    new_edge_rows = jnp.where((counts > 0)[:, None], picked, edge_rows)
    state_rows = jnp.transpose(accepted_states, (1, 0, 2, 3)).reshape(CALLER_TOTAL, ATTENTION_LANES, halves, SLOT_ROWS * LANE_SIZE)
    new_states = jnp.zeros((N_HEAD, SLOTS, SLOT_ROWS * LANE_SIZE), jnp.float32).at[group_ids, targets].set(state_rows)
    new_edges = jnp.zeros((N_HEAD, SLOTS, SLOT_ROWS), jnp.float32).at[group_ids, targets].set(new_edge_rows.reshape(CALLER_TOTAL, ATTENTION_LANES, halves, SLOT_ROWS))
    return (temporal_blend_result, new_states, new_edges)
```

```python
import functools

import jax
import jax.numpy as jnp
from jax import lax
from jax.experimental import pallas as pl
from jax.experimental.pallas import tpu as pltpu
from jax.sharding import PartitionSpec as P

EPSILON = 1e-05
NORM_EPSILON = 0.00064
DECAY_SCALE = 0.6065306597126334

MESH = pl.DeviceIdType.MESH
F32 = jnp.float32
BF16 = jnp.bfloat16
I32 = jnp.int32

NB = 128
NH = 4
REQ = 8
STEPS = 16
WIDTH = 512
HEADS = 8
HW = 64
ROWS = 32
NC = 2
CROWS = ROWS // NC
CW = CROWS * HW
CT = CW // 128
RB = 4

NT = (((1,), (1,)), ((), ()))
TN = (((0,), (0,)), ((), ()))
NN = (((1,), (0,)), ((), ()))


def mm(a, b, dims=NN):
    return lax.dot_general(a, b, dims, preferred_element_type=F32)


def hot(mask):
    return jnp.where(mask, 1.0, 0.0).astype(BF16)


def kernel(
    x_ref, k_ref, v_ref, rq_ref, st_ref, ed_ref,
    ratio_d, ratio_r, off_d, off_r, erase, written, reward, gain, shift,
    left_d, right_d, left_r, right_r,
    dir_ref, tgt_ref, seqv_ref, seq_sm, app_sm,
    tb_ref, ns_ref, ne_ref,
    stag, recv, stag_e, recv_e, back_s, back_r, back_es, back_er,
    r_recv, pb, pr, pb0, pr0,
    hi_s, tr_s, xs, kept, st_t,
    f_r, u_r, a_r, k_r, r_r, r_s, v_r, o_r, bonus_s,
    f_t, u_t, au_t, k_t, r_t, v_t, o_t,
    ss, rs, ss_e, rs_e, ss_b, rs_b, ss_be, rs_be, ss_h, rs_h,
):
    me = lax.axis_index("blk")
    hd = lax.axis_index("head")
    z = lax.div(me, 16)
    y = lax.rem(lax.div(me, 2), 8)
    core = lax.rem(me, 2)
    z_off = [lax.rem(z + i, 8) * 16 for i in range(8)]
    y_off = [lax.rem(y + i, 8) * 2 for i in range(8)]
    c_off = [core, 1 - core]
    far = (4, 3, 5, 2, 6, 1, 7, 0)
    inner = [(b, c) for b in far for c in (1, 0)]

    barrier = pltpu.get_barrier_semaphore()
    for a in far:
        for b, c in inner:
            if a or b or c:
                pl.semaphore_signal(
                    barrier, inc=1, device_id=(z_off[a] + y_off[b] + c_off[c], hd), device_id_type=MESH
                )
    for i in range(1, NH):
        pl.semaphore_signal(barrier, inc=1, device_id=(me, lax.rem(hd + i, NH)), device_id_type=MESH)

    def to_all(src, dst, send_sem, recv_sem):
        def start(d):
            pltpu.make_async_remote_copy(
                src_ref=src.at[d], dst_ref=dst.at[me], send_sem=send_sem, recv_sem=recv_sem,
                device_id=(d, hd), device_id_type=MESH,
            ).start()

        def ring(a, carry):
            dz = 4 + lax.div(a + 1, 2) * (1 - 2 * lax.rem(a, 2))
            base = lax.rem(z + dz, 8) * 16
            for b, c in inner:
                start(base + y_off[b] + c_off[c])
            return carry

        lax.fori_loop(0, 7, ring, 0)
        for b, c in inner[:-1]:
            start(z_off[0] + y_off[b] + c_off[c])

    def all_of(src, dst, send_sem, recv_sem):
        return pltpu.make_async_remote_copy(
            src_ref=src.at[pl.ds(0, NB - 1)], dst_ref=dst.at[pl.ds(0, NB - 1)],
            send_sem=send_sem, recv_sem=recv_sem, device_id=(me, hd), device_id_type=MESH,
        )

    lane = lax.broadcasted_iota(I32, (NB, 128), 1)
    sub = lax.broadcasted_iota(I32, (NB, 128), 0)
    lane_f = lane.astype(F32)

    fetch_q = jnp.zeros((2, 1024), I32)
    place_q = jnp.zeros((2, 1024), I32)
    for h in range(HEADS):
        dv = dir_ref[h]
        tv = tgt_ref[h]
        fetch_q = fetch_q + jnp.where((dv >> 7) == me, dv & 127, 0)
        place_q = place_q + jnp.where((tv >> 7) == me, tv & 127, 0)
        hi_s[2 * h : 2 * h + 2, :] = (dv >> 7).astype(F32)
        hi_s[16 + 2 * h : 18 + 2 * h, :] = (tv >> 7).astype(F32)
    both_q = jnp.sum((fetch_q + place_q * 128).astype(F32), axis=0, keepdims=True)
    seq_t = jnp.transpose(seqv_ref[...].astype(F32))
    cols = []
    for s in range(8):
        col = jnp.broadcast_to(seq_t[:, s : s + 1], (128, 128))
        acc = jnp.zeros((128, 128), F32)
        for qt in range(8):
            acc = acc + jnp.where(
                col == lane_f + float(128 * qt), both_q[:, qt * 128 : (qt + 1) * 128], 0.0
            )
        grouped = jnp.sum(acc.reshape(16, 8, 128), axis=1)
        cols.append(jnp.sum(grouped, axis=1, keepdims=True))
    both = jnp.concatenate(cols, axis=0)
    place = jnp.floor(both * (1.0 / 128.0))
    fetch = both - 128.0 * place
    pick = hot(fetch == lane_f)
    put = hot(place == lane_f)

    row8 = lax.broadcasted_iota(I32, (REQ, 1024), 0)
    lane1024 = lax.broadcasted_iota(I32, (REQ, 1024), 1)
    q_of = jnp.zeros((REQ, 1024), I32)
    count_row = jnp.zeros((1, 128), I32)
    count_col = jnp.zeros((REQ, WIDTH), I32)
    lane1 = lax.broadcasted_iota(I32, (1, 128), 1)
    row8w = lax.broadcasted_iota(I32, (REQ, WIDTH), 0)
    for i in range(REQ):
        q = seq_sm[me * REQ + i]
        n = app_sm[q]
        q_of = jnp.where(row8 == i, q, q_of)
        count_row = jnp.where(lax.rem(lane1, 8) == i, n, count_row)
        count_col = jnp.where(row8w == i, n, count_col)
    own = jnp.where(q_of == lane1024, 1.0, 0.0)
    own = jnp.concatenate([own] * 16, axis=0).astype(BF16)
    spread = mm(hi_s[...].astype(BF16), own, NT)
    r_id = lax.broadcasted_iota(I32, (16, 128), 0)
    l_id = lax.broadcasted_iota(I32, (16, 128), 1)
    group = lax.rem(r_id, 2) * 8 + lax.rem(lax.div(r_id, 2), 2) * 4 + lax.div(r_id, 4)
    mine = lax.div(l_id, 8) == group
    holder = jnp.sum(jnp.where(mine, spread[:16], 0.0), axis=0, keepdims=True)
    owner = jnp.sum(jnp.where(mine, spread[16:], 0.0), axis=0, keepdims=True)
    sub_f = sub.astype(F32)
    from_holder = hot(sub_f == holder)
    to_owner = hot(sub_f == owner)

    edges = jnp.concatenate([ed_ref[...], jnp.zeros((96, 128), F32)], axis=0).astype(BF16)
    stag_e[...] = mm(pick, edges, NT).reshape(NB, 1, 128)

    def lay(dst, src):
        for c in range(CT):
            tr_s[pl.ds(c, NB, stride=CT), :] = src[:, c * 128 : (c + 1) * 128]
        dst[...] = tr_s[...].reshape(NB, CT, 128).astype(BF16)

    def unlay(src):
        tr_s[...] = src[...].astype(F32).reshape(NB * CT, 128)

    for cc in range(NC):
        lay(stag.at[cc], mm(pick, st_ref[:, cc * CW : (cc + 1) * CW].astype(BF16)))

    pl.semaphore_wait(barrier, NB - 1 + NH - 1)
    to_all(stag_e, recv_e, ss_e.at[0], rs_e.at[0])

    def to_heads(src, dst, n):
        for i in range(1, NH):
            pltpu.make_async_remote_copy(
                src_ref=src(lax.rem(hd + i, NH)), dst_ref=dst.at[hd], send_sem=ss_h.at[n], recv_sem=rs_h.at[n],
                device_id=(me, lax.rem(hd + i, NH)), device_id_type=MESH,
            ).start()

    def heads_of(dst, n):
        return pltpu.make_async_remote_copy(
            src_ref=dst.at[pl.ds(0, NH - 1)], dst_ref=dst.at[pl.ds(0, NH - 1)],
            send_sem=ss_h.at[n], recv_sem=rs_h.at[n], device_id=(me, hd), device_id_type=MESH,
        )

    def part(g):
        return rq_ref.at[:, :, pl.ds(pl.multiple_of(g * WIDTH, WIDTH), WIDTH)]

    to_heads(part, r_recv, 0)

    xf = x_ref[...].astype(F32)
    xs[:, 8:24, :] = xf
    xs[:, 0:8, :] = jnp.zeros((REQ, 8, WIDTH), F32)
    prev = xs[:, 7:23, :]
    pb[...] = jnp.zeros(pb.shape, F32)

    def mix(cur, before, ratio):
        return (cur + (before - cur) * ratio).astype(BF16)

    delta_rows = (REQ * STEPS, WIDTH)
    md = mix(xf, prev, ratio_d[...].reshape(1, 1, WIDTH)).reshape(delta_rows)
    mr = mix(xf, prev, ratio_r[...].reshape(1, 1, WIDTH)).reshape(delta_rows)
    pb[0, :, 0:96] = mm(md, left_d[...], NT)
    pb[1, :, 0:96] = mm(mr, left_r[...], NT)
    to_heads(lambda g: pb, pr, 1)

    for cc in range(NC):
        to_all(stag.at[cc], recv.at[cc], ss.at[cc], rs.at[cc])
    recv_e[pl.ds(me, 1)] = stag_e[pl.ds(me, 1)]
    for cc in range(NC):
        recv[cc, pl.ds(me, 1)] = stag[cc, pl.ds(me, 1)]

    pr[pl.ds(hd, 1)] = pb[...].reshape(1, 2, NB, 128)
    r_recv[pl.ds(hd, 1)] = rq_ref[:, :, pl.ds(pl.multiple_of(hd * WIDTH, WIDTH), WIDTH)].reshape(
        1, REQ, 4, WIDTH
    )
    heads_of(r_recv, 0).wait_recv()
    for g in range(NH):
        r_r[:, 4 * g : 4 * g + 4, :] = r_recv[g].astype(F32)

    def put_rows(ref, val):
        for p in range(4):
            ref[p] = val[:, p * 128 : (p + 1) * 128]

    def get_rows(ref):
        return jnp.concatenate([ref[p] for p in range(4)], axis=1)

    def put_step(ref, t, val):
        for p in range(4):
            ref[p, pl.ds(t, REQ, stride=STEPS), :] = val[:, p * 128 : (p + 1) * 128]

    def second(summed_d, summed_r):
        hidden = jnp.tanh(summed_d[:, :96]).astype(BF16)
        zz = off_d[...] + mm(hidden, right_d[...])
        keep = jnp.exp(-DECAY_SCALE * jax.nn.sigmoid(zz))
        rate = jax.nn.sigmoid(off_r[...] + mm(summed_r[:, :96].astype(BF16), right_r[...]))
        return keep, rate

    kf = k_ref[...].astype(F32).reshape(delta_rows)
    put_rows(u_r, kf * erase[...])
    put_rows(v_r, v_ref[...].astype(F32).reshape(delta_rows))
    put_rows(r_s, r_r[...].reshape(delta_rows))

    heads_of(pr, 1).wait_recv()
    keep, rate = second(
        pr[0, 0] + pr[1, 0] + pr[2, 0] + pr[3, 0], pr[0, 1] + pr[1, 1] + pr[2, 1] + pr[3, 1]
    )
    put_rows(f_r, keep)
    put_rows(a_r, rate)
    put_rows(k_r, kf * (1.0 + (rate - 1.0) * written[...]))

    def turn(ref, tp):
        first = [ref[p, pl.ds(2 * tp, REQ, stride=STEPS), :] for p in range(4)]
        other = [ref[p, pl.ds(2 * tp + 1, REQ, stride=STEPS), :] for p in range(4)]
        rows = []
        for at in (0, 64):
            for p in range(4):
                rows.append(jnp.concatenate([first[p][:, at : at + 64], other[p][:, at : at + 64]], axis=1))
        return jnp.transpose(jnp.concatenate(rows + rows, axis=0))

    def turn_pair(tp, carry):
        def put_pair(dst, val):
            dst[pl.ds(2 * tp, 2)] = val.reshape(2, HW, 128)

        put_pair(f_t, turn(f_r, tp))
        put_pair(k_t, turn(k_r, tp))
        put_pair(r_t, turn(r_s, tp))
        u = turn(u_r, tp).reshape(2, HW, 128)
        u = u * lax.rsqrt(jnp.sum(u * u, axis=1, keepdims=True) + EPSILON)
        u_t[pl.ds(2 * tp, 2)] = u
        au_t[pl.ds(2 * tp, 2)] = turn(a_r, tp).reshape(2, HW, 128) * u
        return carry

    def turn_values(tq, carry):
        steps = [[v_r[p, pl.ds(4 * tq + i, REQ, stride=STEPS), :] for p in range(4)] for i in range(4)]
        rows = []
        for half in range(2):
            for odd in range(2):
                for p in range(4):
                    at = odd * 64 + half * 32
                    rows.append(jnp.concatenate([s[p][:, at : at + 32] for s in steps], axis=1))
        v_t[pl.ds(4 * tq, 4)] = jnp.transpose(jnp.concatenate(rows, axis=0)).reshape(4, ROWS, 128)
        return carry

    lax.fori_loop(0, 4, turn_values, 0)
    lax.fori_loop(1, 8, turn_pair, 0)

    all_of(stag_e, recv_e, ss_e.at[0], rs_e.at[0]).wait_recv()
    by_item = mm(from_holder, recv_e[...].reshape(NB, 128).astype(BF16), TN)
    edge_cols = []
    for p in range(4):
        parts = []
        for odd in range(2):
            for half in range(2):
                at = half * 64 + odd * 32 + p * 8
                parts.append(by_item[at : at + 8, 0:32])
        edge_cols.append(jnp.concatenate(parts, axis=1))
    edge = jnp.concatenate(edge_cols, axis=1)
    x0 = xs[:, 8, :]
    pb0[...] = jnp.zeros(pb0.shape, F32)
    pb0[0, :, 0:96] = mm(mix(x0, edge, ratio_d[...]), left_d[...], NT)
    pb0[1, :, 0:96] = mm(mix(x0, edge, ratio_r[...]), left_r[...], NT)
    to_heads(lambda g: pb0, pr0, 2)
    pr0[pl.ds(hd, 1)] = pb0[...].reshape(1, 2, REQ, 128)

    new_edge = jnp.where(count_col == 0, edge, 0.0)
    for t in range(STEPS):
        new_edge = new_edge + jnp.where(count_col == t + 1, xs[:, 8 + t, :], 0.0)
    items = []
    for half in range(2):
        for odd in range(2):
            for p in range(4):
                at = p * 128 + odd * 64 + half * 32
                items.append(new_edge[:, at : at + 32])
    items = jnp.concatenate(items, axis=0)
    items = jnp.concatenate([items, jnp.zeros((NB, 96), F32)], axis=1)
    back_es[...] = mm(to_owner, items.astype(BF16)).reshape(NB, 1, 128)
    to_all(back_es, back_er, ss_be.at[0], rs_be.at[0])
    back_er[pl.ds(me, 1)] = back_es[pl.ds(me, 1)]

    heads_of(pr0, 2).wait_recv()
    keep0, rate0 = second(
        pr0[0, 0] + pr0[1, 0] + pr0[2, 0] + pr0[3, 0], pr0[0, 1] + pr0[1, 1] + pr0[2, 1] + pr0[3, 1]
    )
    k0 = k_ref[...].astype(F32)[:, 0, :]
    put_step(f_r, 0, keep0)
    put_step(a_r, 0, rate0)
    put_step(k_r, 0, k0 * (1.0 + (rate0 - 1.0) * written[...]))
    turn_pair(0, 0)

    def advance_rows(row0, local0):
        start = [st_t[pl.ds(pl.multiple_of((local0 + i) * HW, HW), HW), :] for i in range(RB)]
        for i in range(RB):
            kept[pl.ds(pl.multiple_of((local0 + i) * HW, HW), HW), :] = start[i]

        def step(t, states):
            u, f, au, kk, r = u_t[t], f_t[t], au_t[t], k_t[t], r_t[t]
            taken = jnp.broadcast_to(count_row == t + 1, (HW, 128))
            out = []
            for i in range(RB):
                s = states[i]
                v = v_t[t, pl.ds(row0 + i, 1), :]
                proj = jnp.sum(s * u, axis=0, keepdims=True)
                s = s * f - proj * au + v * kk
                o_t[t, pl.ds(row0 + i, 1), :] = jnp.sum(s * r, axis=0, keepdims=True)
                where = pl.ds(pl.multiple_of((local0 + i) * HW, HW), HW)
                kept[where, :] = jnp.where(taken, s, kept[where, :])
                out.append(s)
            return tuple(out)

        lax.fori_loop(0, STEPS, step, tuple(start))

    for cc in range(NC):
        all_of(stag.at[cc], recv.at[cc], ss.at[cc], rs.at[cc]).wait_recv()
        unlay(recv.at[cc])
        for c in range(CT):
            block = tr_s[pl.ds(c, NB, stride=CT), :].astype(BF16)
            st_t[c * 128 : (c + 1) * 128, :] = mm(block, from_holder, TN)

        def rows(ib, carry):
            advance_rows(cc * CROWS + ib * RB, ib * RB)
            return carry

        lax.fori_loop(0, CROWS // RB, rows, 0)
        lay(back_s.at[cc], mm(to_owner, kept[...].astype(BF16), NT))
        to_all(back_s.at[cc], back_r.at[cc], ss_b.at[cc], rs_b.at[cc])
        back_r[cc, pl.ds(me, 1)] = back_s[cc, pl.ds(me, 1)]

    product = get_rows(r_s) * get_rows(k_r) * reward[...]
    high = product.astype(BF16)
    low = (product - high.astype(F32)).astype(BF16)
    b_row = lax.broadcasted_iota(I32, (WIDTH, WIDTH), 0)
    b_col = lax.broadcasted_iota(I32, (WIDTH, WIDTH), 1)
    same = hot(lax.div(b_row, HW) == lax.div(b_col, HW))
    bonus_s[...] = (mm(high, same) + mm(low, same)) * get_rows(v_r)

    def finish(tq, carry):
        o = o_t[pl.ds(4 * tq, 4)]
        total = jnp.sum(o, axis=1)
        mean = (total + pltpu.roll(total, 64, 1)) * (1.0 / HW)
        cen = o - mean.reshape(4, 1, 128)
        square = jnp.sum(cen * cen, axis=1)
        var = (square + pltpu.roll(square, 64, 1)) * (1.0 / HW)
        norm = cen * lax.rsqrt(var + NORM_EPSILON).reshape(4, 1, 128)
        flat = jnp.transpose(norm.reshape(128, 128))
        for i in range(4):
            pieces = []
            for p in range(4):
                for odd in range(2):
                    for half in range(2):
                        at = half * 64 + odd * 32 + p * 8
                        pieces.append(flat[at : at + 8, i * 32 : (i + 1) * 32])
            put_step(o_r, 4 * tq + i, jnp.concatenate(pieces, axis=1))
        return carry

    lax.fori_loop(0, 4, finish, 0)
    result = get_rows(o_r) * gain[...] + shift[...] + bonus_s[...]
    tb_ref[...] = result.astype(BF16).reshape(REQ, STEPS, WIDTH)

    all_of(back_es, back_er, ss_be.at[0], rs_be.at[0]).wait_recv()
    ne_ref[...] = mm(back_er[...].reshape(NB, 128).astype(BF16), put, TN)[0:32]
    for cc in range(NC):
        all_of(back_s.at[cc], back_r.at[cc], ss_b.at[cc], rs_b.at[cc]).wait_recv()
        unlay(back_r.at[cc])
        for c in range(CT):
            block = tr_s[pl.ds(c, NB, stride=CT), :].astype(BF16)
            at = cc * CW + c * 128
            ns_ref[:, at : at + 128] = mm(put, block, TN)

    all_of(stag_e, recv_e, ss_e.at[0], rs_e.at[0]).wait_send()
    all_of(back_es, back_er, ss_be.at[0], rs_be.at[0]).wait_send()
    for cc in range(NC):
        all_of(stag.at[cc], recv.at[cc], ss.at[cc], rs.at[cc]).wait_send()
        all_of(back_s.at[cc], back_r.at[cc], ss_b.at[cc], rs_b.at[cc]).wait_send()
    heads_of(r_recv, 0).wait_send()
    heads_of(pr, 1).wait_send()
    heads_of(pr0, 2).wait_send()


def local(
    layer_entry_vectors, guessed_lookup_vectors, guessed_content_vectors, gating_query,
    lane_memory_store, prior_step_store, fading_blend_ratio, learning_speed_blend,
    fading_left_factor, fading_right_factor, fading_offset,
    learning_speed_left, learning_speed_right, learning_speed_offset,
    erasing_lookup_factor, written_lookup_factor, present_reward_factors,
    lane_standard_factor, lane_standard_offset,
    caller_memory_directory, kept_target_place, caller_sequence, approved_guesses,
):
    def row(vector):
        return vector.reshape(1, WIDTH)

    vmem = pl.BlockSpec(memory_space=pltpu.VMEM)
    smem = pl.BlockSpec(memory_space=pltpu.SMEM)
    dma = pltpu.SemaphoreType.DMA
    rows = REQ * STEPS
    outs = pl.pallas_call(
        kernel,
        out_shape=(
            jax.ShapeDtypeStruct((REQ, STEPS, WIDTH), BF16),
            jax.ShapeDtypeStruct((NB, 2048), F32),
            jax.ShapeDtypeStruct((32, NB), F32),
        ),
        in_specs=[vmem] * 22 + [smem] * 2,
        out_specs=(vmem, vmem, vmem),
        scratch_shapes=[
            pltpu.VMEM((NC, NB, CT, 128), BF16),
            pltpu.VMEM((NC, NB, CT, 128), BF16),
            pltpu.VMEM((NB, 1, 128), F32),
            pltpu.VMEM((NB, 1, 128), F32),
            pltpu.VMEM((NC, NB, CT, 128), BF16),
            pltpu.VMEM((NC, NB, CT, 128), BF16),
            pltpu.VMEM((NB, 1, 128), F32),
            pltpu.VMEM((NB, 1, 128), F32),
            pltpu.VMEM((NH, REQ, 4, WIDTH), BF16),
            pltpu.VMEM((2, NB, 128), F32),
            pltpu.VMEM((NH, 2, NB, 128), F32),
            pltpu.VMEM((2, REQ, 128), F32),
            pltpu.VMEM((NH, 2, REQ, 128), F32),
            pltpu.VMEM((32, 1024), F32),
            pltpu.VMEM((NB * CT, 128), F32),
            pltpu.VMEM((REQ, 24, WIDTH), F32),
            pltpu.VMEM((CW, 128), F32),
            pltpu.VMEM((CW, 128), F32),
            pltpu.VMEM((4, rows, 128), F32),
            pltpu.VMEM((4, rows, 128), F32),
            pltpu.VMEM((4, rows, 128), F32),
            pltpu.VMEM((4, rows, 128), F32),
            pltpu.VMEM((REQ, STEPS, WIDTH), F32),
            pltpu.VMEM((4, rows, 128), F32),
            pltpu.VMEM((4, rows, 128), F32),
            pltpu.VMEM((4, rows, 128), F32),
            pltpu.VMEM((rows, WIDTH), F32),
            pltpu.VMEM((STEPS, HW, 128), F32),
            pltpu.VMEM((STEPS, HW, 128), F32),
            pltpu.VMEM((STEPS, HW, 128), F32),
            pltpu.VMEM((STEPS, HW, 128), F32),
            pltpu.VMEM((STEPS, HW, 128), F32),
            pltpu.VMEM((STEPS, ROWS, 128), F32),
            pltpu.VMEM((STEPS, ROWS, 128), F32),
            dma((NC,)), dma((NC,)), dma((1,)), dma((1,)),
            dma((NC,)), dma((NC,)), dma((1,)), dma((1,)), dma((3,)), dma((3,)),
        ],
        compiler_params=pltpu.CompilerParams(
            collective_id=0, has_side_effects=True, vmem_limit_bytes=56 << 20
        ),
        name="draft_check",
    )(
        layer_entry_vectors, guessed_lookup_vectors, guessed_content_vectors, gating_query,
        lane_memory_store.reshape(NB, 2048), jnp.transpose(prior_step_store[0]),
        row(fading_blend_ratio), row(learning_speed_blend), row(fading_offset), row(learning_speed_offset),
        row(erasing_lookup_factor), row(written_lookup_factor), row(present_reward_factors),
        row(lane_standard_factor), row(lane_standard_offset),
        jnp.transpose(fading_left_factor), fading_right_factor,
        jnp.transpose(learning_speed_left), learning_speed_right,
        jnp.transpose(caller_memory_directory, (1, 2, 0)), jnp.transpose(kept_target_place, (1, 2, 0)),
        caller_sequence.reshape(8, 128), caller_sequence, approved_guesses,
    )
    return (outs[0], outs[1][None], jnp.transpose(outs[2])[None])


def solution(mesh):
    return jax.shard_map(
        local,
        mesh=mesh,
        in_specs=(
            P("blk", None, "head"), P("blk", None, "head"), P("blk", None, "head"), P("blk", "head", None),
            P("head", "blk", None), P("head", "blk", None),
            P("head"), P("head"), P("head", None), P(None, "head"), P("head"),
            P("head", None), P(None, "head"), P("head"),
            P("head"), P("head"), P("head"), P("head"), P("head"),
            P(None, "head", None), P(None, "head", None), P(), P(),
        ),
        out_specs=(P("blk", None, "head"), P("head", "blk", None), P("head", "blk", None)),
        check_vma=False,
    )
```

```python
import functools

import jax
import jax.numpy as jnp
from jax import lax
from jax.experimental import pallas as pl
from jax.experimental.pallas import tpu as pltpu
from jax.sharding import PartitionSpec as P

EPSILON = 1e-05
NORM_EPSILON = 0.00064
DECAY_SCALE = 0.6065306597126334

MESH = pl.DeviceIdType.MESH
F32 = jnp.float32
BF16 = jnp.bfloat16
I32 = jnp.int32

NB = 128
NH = 4
REQ = 8
STEPS = 16
WIDTH = 512
HEADS = 8
HW = 64
ROWS = 32
NI = 24
NC = 4
CROWS = ROWS // NC
CW = CROWS * HW
CT = CW // 128
RB = 4

NT = (((1,), (1,)), ((), ()))
TN = (((0,), (0,)), ((), ()))
NN = (((1,), (0,)), ((), ()))


def mm(a, b, dims=NN):
    return lax.dot_general(a, b, dims, preferred_element_type=F32)


def hot(mask):
    return jnp.where(mask, 1.0, 0.0).astype(BF16)


def kernel(*refs):
    hbm, (tb_ref, back_r, back_er, put_ref) = refs[:NI], refs[NI : NI + 4]
    held, ss_i = refs[NI + 4 : 2 * NI + 4], refs[2 * NI + 4]
    loads = [pltpu.make_async_copy(hbm[i], held[i], ss_i.at[i]) for i in range(NI)]
    for i in (21, 19, 20, 22, 23, 4, 5, 3, 0, 1, 2) + tuple(range(6, 19)):
        loads[i].start()
    (
        x_ref, k_ref, v_ref, rq_ref, st_ref, ed_ref,
        ratio_d, ratio_r, off_d, off_r, erase, written, reward, gain, shift,
        left_d, right_d, left_r, right_r, dir_ref, tgt_ref, seqv_ref, seq_sm, app_sm,
    ) = held
    (
        stag, mid, recv, stag_e, mid_e, recv_e, back_s, back_m, back_es, back_em,
        r_recv, pb, pr, pb0, pr0,
        hi_s, tr_s, xs, kept, st_t,
        f_r, u_r, a_r, k_r, r_r, r_s, v_r, o_r, bonus_s,
        f_t, u_t, au_t, k_t, r_t, v_t, o_t,
        ss_e, rs_e, ss_h, rs_h,
    ) = refs[2 * NI + 5 :]
    me = lax.axis_index("blk")
    hd = lax.axis_index("head")
    z = lax.div(me, 16)
    y = lax.rem(lax.div(me, 2), 8)
    core = lax.rem(me, 2)
    z_off = [lax.rem(z + i, 8) * 16 for i in range(8)]
    y_off = [lax.rem(y + i, 8) * 2 for i in range(8)]
    c_off = [core, 1 - core]
    far = (4, 3, 5, 2, 6, 1, 7, 0)
    inner = [(b, c) for b in far for c in (1, 0)]

    barrier = pltpu.get_barrier_semaphore()
    for a in far[:-1]:
        pl.semaphore_signal(
            barrier, inc=1, device_id=(z_off[a] + lax.rem(me, 16), hd), device_id_type=MESH
        )
    for b, c in inner[:-1]:
        pl.semaphore_signal(
            barrier, inc=1, device_id=(z_off[0] + y_off[b] + c_off[c], hd), device_id_type=MESH
        )
    for i in range(1, NH):
        pl.semaphore_signal(barrier, inc=1, device_id=(me, lax.rem(hd + i, NH)), device_id_type=MESH)

    lane = lax.broadcasted_iota(I32, (NB, 128), 1)
    sub = lax.broadcasted_iota(I32, (NB, 128), 0)
    lane_f = lane.astype(F32)

    w = lax.rem(me, 16)

    def hop_z(src, dst, n):
        for a in far[:-1]:
            pltpu.make_async_remote_copy(
                src_ref=src.at[lax.rem(z + a, 8)], dst_ref=dst.at[z], send_sem=ss_e.at[n], recv_sem=rs_e.at[n],
                device_id=(z_off[a] + w, hd), device_id_type=MESH,
            ).start()
        dst[pl.ds(z, 1)] = src[pl.ds(z, 1)]

    def hop_w(src, dst, n):
        for b, c in inner[:-1]:
            to = y_off[b] + c_off[c]
            pltpu.make_async_remote_copy(
                src_ref=src.at[:, to], dst_ref=dst.at[:, w], send_sem=ss_e.at[n], recv_sem=rs_e.at[n],
                device_id=(z_off[0] + to, hd), device_id_type=MESH,
            ).start()
        dst[:, pl.ds(w, 1)] = src[:, pl.ds(w, 1)]

    def all_z(src, dst, n):
        return pltpu.make_async_remote_copy(
            src_ref=src.at[pl.ds(0, 7)], dst_ref=dst.at[pl.ds(0, 7)],
            send_sem=ss_e.at[n], recv_sem=rs_e.at[n], device_id=(me, hd), device_id_type=MESH,
        )

    def all_w(src, dst, n):
        return pltpu.make_async_remote_copy(
            src_ref=src.at[:, pl.ds(0, 15)], dst_ref=dst.at[:, pl.ds(0, 15)],
            send_sem=ss_e.at[n], recv_sem=rs_e.at[n], device_id=(me, hd), device_id_type=MESH,
        )

    for i in (21, 19, 20, 22, 23):
        loads[i].wait()

    fetch_q = jnp.zeros((2, 1024), I32)
    place_q = jnp.zeros((2, 1024), I32)
    for h in range(HEADS):
        dv = dir_ref[h]
        tv = tgt_ref[h]
        fetch_q = fetch_q + jnp.where((dv >> 7) == me, dv & 127, 0)
        place_q = place_q + jnp.where((tv >> 7) == me, tv & 127, 0)
        hi_s[2 * h : 2 * h + 2, :] = (dv >> 7).astype(F32)
        hi_s[16 + 2 * h : 18 + 2 * h, :] = (tv >> 7).astype(F32)
    both_q = jnp.sum((fetch_q + place_q * 128).astype(F32), axis=0, keepdims=True)
    seq_t = jnp.transpose(seqv_ref[...].astype(F32))
    cols = []
    for s in range(8):
        col = jnp.broadcast_to(seq_t[:, s : s + 1], (128, 128))
        acc = jnp.zeros((128, 128), F32)
        for qt in range(8):
            acc = acc + jnp.where(
                col == lane_f + float(128 * qt), both_q[:, qt * 128 : (qt + 1) * 128], 0.0
            )
        grouped = jnp.sum(acc.reshape(16, 8, 128), axis=1)
        cols.append(jnp.sum(grouped, axis=1, keepdims=True))
    both = jnp.concatenate(cols, axis=0)
    place = jnp.floor(both * (1.0 / 128.0))
    fetch = both - 128.0 * place
    pick = hot(fetch == lane_f)
    put_ref[...] = hot(place == lane_f)

    row8 = lax.broadcasted_iota(I32, (REQ, 1024), 0)
    lane1024 = lax.broadcasted_iota(I32, (REQ, 1024), 1)
    q_of = jnp.zeros((REQ, 1024), I32)
    count_row = jnp.zeros((1, 128), I32)
    count_col = jnp.zeros((REQ, WIDTH), I32)
    lane1 = lax.broadcasted_iota(I32, (1, 128), 1)
    row8w = lax.broadcasted_iota(I32, (REQ, WIDTH), 0)
    for i in range(REQ):
        q = seq_sm[me * REQ + i]
        n = app_sm[q]
        q_of = jnp.where(row8 == i, q, q_of)
        count_row = jnp.where(lax.rem(lane1, 8) == i, n, count_row)
        count_col = jnp.where(row8w == i, n, count_col)
    own = jnp.where(q_of == lane1024, 1.0, 0.0)
    own = jnp.concatenate([own] * 16, axis=0).astype(BF16)
    spread = mm(hi_s[...].astype(BF16), own, NT)
    r_id = lax.broadcasted_iota(I32, (16, 128), 0)
    l_id = lax.broadcasted_iota(I32, (16, 128), 1)
    group = lax.rem(r_id, 2) * 8 + lax.rem(lax.div(r_id, 2), 2) * 4 + lax.div(r_id, 4)
    mine = lax.div(l_id, 8) == group
    holder = jnp.sum(jnp.where(mine, spread[:16], 0.0), axis=0, keepdims=True)
    owner = jnp.sum(jnp.where(mine, spread[16:], 0.0), axis=0, keepdims=True)
    sub_f = sub.astype(F32)
    from_holder = hot(sub_f == holder)
    to_owner = hot(sub_f == owner)

    loads[4].wait()
    loads[5].wait()
    edges = jnp.concatenate([ed_ref[...], jnp.zeros((96, 128), F32)], axis=0).astype(BF16)
    stag_e[...] = mm(pick, edges, NT).reshape(8, 16, 1, 128)

    def lay(dst, src, ct):
        for c in range(ct):
            tr_s[pl.ds(c, NB, stride=ct), :] = src[:, c * 128 : (c + 1) * 128]
        dst[...] = tr_s[pl.ds(0, NB * ct), :].reshape(dst.shape).astype(BF16)

    for cc in range(NC):
        lay(stag.at[cc], mm(pick, st_ref[:, cc * CW : (cc + 1) * CW].astype(BF16)), CT)

    def first_hop(src, dst, cc, n):
        (hop_w if cc % 2 else hop_z)(src.at[cc], dst.at[cc], n + 2 * cc)

    def first_all(src, dst, cc, n):
        return (all_w if cc % 2 else all_z)(src.at[cc], dst.at[cc], n + 2 * cc)

    def second_hop(src, dst, cc, n):
        (hop_z if cc % 2 else hop_w)(src.at[cc], dst.at[cc], n + 1 + 2 * cc)

    def second_all(src, dst, cc, n):
        return (all_z if cc % 2 else all_w)(src.at[cc], dst.at[cc], n + 1 + 2 * cc)

    fetch_n, back_n = 4, 4 + 2 * NC

    for i in (3, 0, 1, 2) + tuple(range(6, 19)):
        loads[i].wait()
    xf = x_ref[...].astype(F32)
    xs[:, 8:24, :] = xf
    xs[:, 0:8, :] = jnp.zeros((REQ, 8, WIDTH), F32)
    prev = xs[:, 7:23, :]

    def mix(cur, before, ratio):
        return (cur + (before - cur) * ratio).astype(BF16)

    delta_rows = (REQ * STEPS, WIDTH)
    md = mix(xf, prev, ratio_d[...].reshape(1, 1, WIDTH)).reshape(delta_rows)
    mr = mix(xf, prev, ratio_r[...].reshape(1, 1, WIDTH)).reshape(delta_rows)
    pb[0] = mm(left_d[...], md, NT).astype(BF16)
    pb[1] = mm(left_r[...], mr, NT).astype(BF16)
    def to_heads(src, dst, n):
        for i in range(1, NH):
            pltpu.make_async_remote_copy(
                src_ref=src(lax.rem(hd + i, NH)), dst_ref=dst.at[hd], send_sem=ss_h.at[n], recv_sem=rs_h.at[n],
                device_id=(me, lax.rem(hd + i, NH)), device_id_type=MESH,
            ).start()

    def heads_of(dst, n):
        return pltpu.make_async_remote_copy(
            src_ref=dst.at[pl.ds(0, NH - 1)], dst_ref=dst.at[pl.ds(0, NH - 1)],
            send_sem=ss_h.at[n], recv_sem=rs_h.at[n], device_id=(me, hd), device_id_type=MESH,
        )

    def part(g):
        return rq_ref.at[:, :, pl.ds(pl.multiple_of(g * WIDTH, WIDTH), WIDTH)]

    pl.semaphore_wait(barrier, 7 + 15 + NH - 1)
    hop_z(stag_e, mid_e, 0)
    to_heads(part, r_recv, 0)
    to_heads(lambda g: pb, pr, 1)
    first_hop(stag, mid, 0, fetch_n)
    first_hop(stag, mid, 1, fetch_n)

    pr[pl.ds(hd, 1)] = pb[...].reshape(1, 2, 96, 128)
    r_recv[pl.ds(hd, 1)] = rq_ref[:, :, pl.ds(pl.multiple_of(hd * WIDTH, WIDTH), WIDTH)].reshape(
        1, REQ, 4, WIDTH
    )
    heads_of(r_recv, 0).wait_recv()
    for g in range(NH):
        r_r[:, 4 * g : 4 * g + 4, :] = r_recv[g].astype(F32)

    def put_rows(ref, val):
        for p in range(4):
            ref[p] = val[:, p * 128 : (p + 1) * 128]

    def get_rows(ref):
        return jnp.concatenate([ref[p] for p in range(4)], axis=1)

    def put_step(ref, t, val):
        for p in range(4):
            ref[p, pl.ds(t, REQ, stride=STEPS), :] = val[:, p * 128 : (p + 1) * 128]

    def second(summed_d, summed_r, dims):
        hidden = jnp.tanh(summed_d).astype(BF16)
        zz = off_d[...] + mm(hidden, right_d[...], dims)
        keep = jnp.exp(-DECAY_SCALE * jax.nn.sigmoid(zz))
        rate = jax.nn.sigmoid(off_r[...] + mm(summed_r.astype(BF16), right_r[...], dims))
        return keep, rate

    kf = k_ref[...].astype(F32).reshape(delta_rows)
    put_rows(u_r, kf * erase[...])
    put_rows(v_r, v_ref[...].astype(F32).reshape(delta_rows))
    put_rows(r_s, r_r[...].reshape(delta_rows))

    heads_of(pr, 1).wait_recv()
    sums = pr[0].astype(F32) + pr[1].astype(F32) + pr[2].astype(F32) + pr[3].astype(F32)
    keep, rate = second(sums[0], sums[1], TN)
    put_rows(f_r, keep)
    put_rows(a_r, rate)
    put_rows(k_r, kf * (1.0 + (rate - 1.0) * written[...]))

    def turn(ref, tp):
        first = [ref[p, pl.ds(2 * tp, REQ, stride=STEPS), :] for p in range(4)]
        other = [ref[p, pl.ds(2 * tp + 1, REQ, stride=STEPS), :] for p in range(4)]
        rows = []
        for at in (0, 64):
            for p in range(4):
                rows.append(jnp.concatenate([first[p][:, at : at + 64], other[p][:, at : at + 64]], axis=1))
        return jnp.transpose(jnp.concatenate(rows + rows, axis=0))

    def turn_pair(tp, carry):
        def put_pair(dst, val):
            dst[pl.ds(2 * tp, 2)] = val.reshape(2, HW, 128)

        put_pair(f_t, turn(f_r, tp))
        put_pair(k_t, turn(k_r, tp))
        put_pair(r_t, turn(r_s, tp))
        u = turn(u_r, tp).reshape(2, HW, 128)
        u = u * lax.rsqrt(jnp.sum(u * u, axis=1, keepdims=True) + EPSILON)
        u_t[pl.ds(2 * tp, 2)] = u
        au_t[pl.ds(2 * tp, 2)] = turn(a_r, tp).reshape(2, HW, 128) * u
        return carry

    def turn_values(tq, carry):
        steps = [[v_r[p, pl.ds(4 * tq + i, REQ, stride=STEPS), :] for p in range(4)] for i in range(4)]
        rows = []
        for half in range(2):
            for odd in range(2):
                for p in range(4):
                    at = odd * 64 + half * 32
                    rows.append(jnp.concatenate([s[p][:, at : at + 32] for s in steps], axis=1))
        v_t[pl.ds(4 * tq, 4)] = jnp.transpose(jnp.concatenate(rows, axis=0)).reshape(4, ROWS, 128)
        return carry

    lax.fori_loop(0, 4, turn_values, 0)

    all_z(stag_e, mid_e, 0).wait_recv()
    hop_w(mid_e, recv_e, 1)
    first_hop(stag, mid, 2, fetch_n)
    first_hop(stag, mid, 3, fetch_n)
    lax.fori_loop(1, 8, turn_pair, 0)

    def pass_on(cc):
        first_all(stag, mid, cc, fetch_n).wait_recv()
        second_hop(mid, recv, cc, fetch_n)

    pass_on(0)
    pass_on(1)

    all_w(mid_e, recv_e, 1).wait_recv()
    by_item = mm(from_holder, recv_e[...].reshape(NB, 128).astype(BF16), TN)
    edge_cols = []
    for p in range(4):
        parts = []
        for odd in range(2):
            for half in range(2):
                at = half * 64 + odd * 32 + p * 8
                parts.append(by_item[at : at + 8, 0:32])
        edge_cols.append(jnp.concatenate(parts, axis=1))
    edge = jnp.concatenate(edge_cols, axis=1)
    x0 = xs[:, 8, :]
    pb0[...] = jnp.zeros(pb0.shape, F32)
    pb0[0, :, 0:96] = mm(mix(x0, edge, ratio_d[...]), left_d[...], NT)
    pb0[1, :, 0:96] = mm(mix(x0, edge, ratio_r[...]), left_r[...], NT)
    to_heads(lambda g: pb0, pr0, 2)
    pr0[pl.ds(hd, 1)] = pb0[...].reshape(1, 2, REQ, 128)


    new_edge = jnp.where(count_col == 0, edge, 0.0)
    for t in range(STEPS):
        new_edge = new_edge + jnp.where(count_col == t + 1, xs[:, 8 + t, :], 0.0)
    items = []
    for half in range(2):
        for odd in range(2):
            for p in range(4):
                at = p * 128 + odd * 64 + half * 32
                items.append(new_edge[:, at : at + 32])
    items = jnp.concatenate(items, axis=0)
    items = jnp.concatenate([items, jnp.zeros((NB, 96), F32)], axis=1)
    back_es[...] = mm(to_owner, items.astype(BF16)).reshape(8, 16, 1, 128)
    hop_z(back_es, back_em, 2)

    pass_on(2)
    pass_on(3)
    heads_of(pr0, 2).wait_recv()
    sums0 = (pr0[0] + pr0[1] + pr0[2] + pr0[3])[:, :, :96]
    keep0, rate0 = second(sums0[0], sums0[1], NN)
    k0 = k_ref[...].astype(F32)[:, 0, :]
    put_step(f_r, 0, keep0)
    put_step(a_r, 0, rate0)
    put_step(k_r, 0, k0 * (1.0 + (rate0 - 1.0) * written[...]))
    turn_pair(0, 0)

    def advance_rows(row0, local0):
        start = [st_t[pl.ds(pl.multiple_of((local0 + i) * HW, HW), HW), :] for i in range(RB)]
        for i in range(RB):
            kept[pl.ds(pl.multiple_of((local0 + i) * HW, HW), HW), :] = start[i]

        def step(t, states):
            u, f, au, kk, r = u_t[t], f_t[t], au_t[t], k_t[t], r_t[t]
            taken = jnp.broadcast_to(count_row == t + 1, (HW, 128))
            out = []
            for i in range(RB):
                s = states[i]
                v = v_t[t, pl.ds(row0 + i, 1), :]
                proj = jnp.sum(s * u, axis=0, keepdims=True)
                s = s * f - proj * au + v * kk
                o_t[t, pl.ds(row0 + i, 1), :] = jnp.sum(s * r, axis=0, keepdims=True)
                where = pl.ds(pl.multiple_of((local0 + i) * HW, HW), HW)
                kept[where, :] = jnp.where(taken, s, kept[where, :])
                out.append(s)
            return tuple(out)

        lax.fori_loop(0, STEPS, step, tuple(start))

    def return_on(cc):
        first_all(back_s, back_m, cc, back_n).wait_recv()
        second_hop(back_m, back_r, cc, back_n)

    for cc in range(NC):
        second_all(mid, recv, cc, fetch_n).wait_recv()
        tr_s[...] = recv[cc].astype(F32).reshape(NB * CT, 128)
        for c in range(CT):
            block = tr_s[pl.ds(c, NB, stride=CT), :].astype(BF16)
            st_t[c * 128 : (c + 1) * 128, :] = mm(block, from_holder, TN)

        def rows(ib, carry, cc=cc):
            advance_rows(cc * CROWS + ib * RB, ib * RB)
            return carry

        lax.fori_loop(0, CROWS // RB, rows, 0)
        lay(back_s.at[cc], mm(to_owner, kept[...].astype(BF16), NT), CT)
        first_hop(back_s, back_m, cc, back_n)
        if cc == 0:
            all_z(back_es, back_em, 2).wait_recv()
            hop_w(back_em, back_er, 3)
        if cc >= 2:
            return_on(cc - 2)

    product = get_rows(r_s) * get_rows(k_r) * reward[...]
    high = product.astype(BF16)
    low = (product - high.astype(F32)).astype(BF16)
    b_row = lax.broadcasted_iota(I32, (WIDTH, WIDTH), 0)
    b_col = lax.broadcasted_iota(I32, (WIDTH, WIDTH), 1)
    same = hot(lax.div(b_row, HW) == lax.div(b_col, HW))
    bonus_s[...] = (mm(high, same) + mm(low, same)) * get_rows(v_r)

    return_on(NC - 2)

    def finish(tq, carry):
        o = o_t[pl.ds(4 * tq, 4)]
        total = jnp.sum(o, axis=1)
        mean = (total + pltpu.roll(total, 64, 1)) * (1.0 / HW)
        cen = o - mean.reshape(4, 1, 128)
        square = jnp.sum(cen * cen, axis=1)
        var = (square + pltpu.roll(square, 64, 1)) * (1.0 / HW)
        norm = cen * lax.rsqrt(var + NORM_EPSILON).reshape(4, 1, 128)
        flat = jnp.transpose(norm.reshape(128, 128))
        for i in range(4):
            pieces = []
            for p in range(4):
                for odd in range(2):
                    for half in range(2):
                        at = half * 64 + odd * 32 + p * 8
                        pieces.append(flat[at : at + 8, i * 32 : (i + 1) * 32])
            put_step(o_r, 4 * tq + i, jnp.concatenate(pieces, axis=1))
        return carry

    lax.fori_loop(0, 4, finish, 0)
    return_on(NC - 1)
    result = get_rows(o_r) * gain[...] + shift[...] + bonus_s[...]
    tb_ref[...] = result.astype(BF16).reshape(REQ, STEPS, WIDTH)

    all_w(back_em, back_er, 3).wait_recv()
    for cc in range(NC):
        second_all(back_m, back_r, cc, back_n).wait_recv()
    all_z(stag_e, mid_e, 0).wait_send()
    all_w(mid_e, recv_e, 1).wait_send()
    all_z(back_es, back_em, 2).wait_send()
    all_w(back_em, back_er, 3).wait_send()
    for cc in range(NC):
        first_all(stag, mid, cc, fetch_n).wait_send()
        second_all(mid, recv, cc, fetch_n).wait_send()
        first_all(back_s, back_m, cc, back_n).wait_send()
        second_all(back_m, back_r, cc, back_n).wait_send()
    heads_of(r_recv, 0).wait_send()
    heads_of(pr, 1).wait_send()
    heads_of(pr0, 2).wait_send()


def settle(tb_ref, back_r, back_er, put_ref, out_ref, ns_ref, ne_ref, tr_s):
    out_ref[...] = tb_ref[...]
    put = put_ref[...]
    ne_ref[...] = mm(back_er[...].reshape(NB, 128).astype(BF16), put, TN)[0:32]
    put_t = jnp.transpose(put.astype(F32)).astype(BF16)
    for cc in range(NC):
        tr_s[...] = back_r[cc].astype(F32).reshape(NB * CT, 128)
        for c in range(CT):
            block = tr_s[pl.ds(c, NB, stride=CT), :].astype(BF16)
            at = cc * CW + c * 128
            ns_ref[:, at : at + 128] = mm(put_t, block)


def local(
    layer_entry_vectors, guessed_lookup_vectors, guessed_content_vectors, gating_query,
    lane_memory_store, prior_step_store, fading_blend_ratio, learning_speed_blend,
    fading_left_factor, fading_right_factor, fading_offset,
    learning_speed_left, learning_speed_right, learning_speed_offset,
    erasing_lookup_factor, written_lookup_factor, present_reward_factors,
    lane_standard_factor, lane_standard_offset,
    caller_memory_directory, kept_target_place, caller_sequence, approved_guesses,
):
    def row(vector):
        return vector.reshape(1, WIDTH)

    vmem = pl.BlockSpec(memory_space=pltpu.VMEM)
    dma = pltpu.SemaphoreType.DMA
    rows = REQ * STEPS
    arrays = (
        layer_entry_vectors, guessed_lookup_vectors, guessed_content_vectors, gating_query,
        lane_memory_store.reshape(NB, 2048), jnp.transpose(prior_step_store[0]),
        row(fading_blend_ratio), row(learning_speed_blend), row(fading_offset), row(learning_speed_offset),
        row(erasing_lookup_factor), row(written_lookup_factor), row(present_reward_factors),
        row(lane_standard_factor), row(lane_standard_offset),
        jnp.transpose(fading_left_factor), fading_right_factor,
        jnp.transpose(learning_speed_left), learning_speed_right,
        jnp.transpose(caller_memory_directory, (1, 2, 0)), jnp.transpose(kept_target_place, (1, 2, 0)),
        caller_sequence.reshape(8, 128), caller_sequence, approved_guesses,
    )
    hbm = pl.BlockSpec(memory_space=pltpu.HBM)
    outs = pl.pallas_call(
        kernel,
        out_shape=(
            jax.ShapeDtypeStruct((REQ, STEPS, WIDTH), BF16),
            jax.ShapeDtypeStruct((NC, 8, 16, CT, 128), BF16),
            jax.ShapeDtypeStruct((8, 16, 1, 128), F32),
            jax.ShapeDtypeStruct((NB, 128), BF16),
        ),
        in_specs=[hbm] * NI,
        out_specs=(vmem,) * 4,
        scratch_shapes=[pltpu.VMEM(a.shape, a.dtype) for a in arrays[:-2]]
        + [pltpu.SMEM(a.shape, a.dtype) for a in arrays[-2:]]
        + [
            dma((NI,)),
            pltpu.VMEM((NC, 8, 16, CT, 128), BF16),
            pltpu.VMEM((NC, 8, 16, CT, 128), BF16),
            pltpu.VMEM((NC, 8, 16, CT, 128), BF16),
            pltpu.VMEM((8, 16, 1, 128), F32),
            pltpu.VMEM((8, 16, 1, 128), F32),
            pltpu.VMEM((8, 16, 1, 128), F32),
            pltpu.VMEM((NC, 8, 16, CT, 128), BF16),
            pltpu.VMEM((NC, 8, 16, CT, 128), BF16),
            pltpu.VMEM((8, 16, 1, 128), F32),
            pltpu.VMEM((8, 16, 1, 128), F32),
            pltpu.VMEM((NH, REQ, 4, WIDTH), BF16),
            pltpu.VMEM((2, 96, 128), BF16),
            pltpu.VMEM((NH, 2, 96, 128), BF16),
            pltpu.VMEM((2, REQ, 128), F32),
            pltpu.VMEM((NH, 2, REQ, 128), F32),
            pltpu.VMEM((32, 1024), F32),
            pltpu.VMEM((NB * CT, 128), F32),
            pltpu.VMEM((REQ, 24, WIDTH), F32),
            pltpu.VMEM((CW, 128), F32),
            pltpu.VMEM((CW, 128), F32),
            pltpu.VMEM((4, rows, 128), F32),
            pltpu.VMEM((4, rows, 128), F32),
            pltpu.VMEM((4, rows, 128), F32),
            pltpu.VMEM((4, rows, 128), F32),
            pltpu.VMEM((REQ, STEPS, WIDTH), F32),
            pltpu.VMEM((4, rows, 128), F32),
            pltpu.VMEM((4, rows, 128), F32),
            pltpu.VMEM((4, rows, 128), F32),
            pltpu.VMEM((rows, WIDTH), F32),
            pltpu.VMEM((STEPS, HW, 128), F32),
            pltpu.VMEM((STEPS, HW, 128), F32),
            pltpu.VMEM((STEPS, HW, 128), F32),
            pltpu.VMEM((STEPS, HW, 128), F32),
            pltpu.VMEM((STEPS, HW, 128), F32),
            pltpu.VMEM((STEPS, ROWS, 128), F32),
            pltpu.VMEM((STEPS, ROWS, 128), F32),
            dma((4 + 4 * NC,)), dma((4 + 4 * NC,)), dma((3,)), dma((3,)),
        ],
        compiler_params=pltpu.CompilerParams(
            collective_id=0, has_side_effects=True, vmem_limit_bytes=24 << 20
        ),
        name="draft_check",
    )(
        *[pltpu.with_memory_space_constraint(a, pltpu.HBM) for a in arrays]
    )
    result, states, edges = pl.pallas_call(
        settle,
        out_shape=(
            jax.ShapeDtypeStruct((REQ, STEPS, WIDTH), BF16),
            jax.ShapeDtypeStruct((NB, 2048), F32),
            jax.ShapeDtypeStruct((32, NB), F32),
        ),
        in_specs=[vmem] * 4,
        out_specs=(vmem,) * 3,
        scratch_shapes=[pltpu.VMEM((NB * CT, 128), F32)],
        compiler_params=pltpu.CompilerParams(vmem_limit_bytes=12 << 20),
        name="settle",
    )(*outs)
    return (result, states[None], jnp.transpose(edges)[None])


def solution(mesh):
    return jax.shard_map(
        local,
        mesh=mesh,
        in_specs=(
            P("blk", None, "head"), P("blk", None, "head"), P("blk", None, "head"), P("blk", "head", None),
            P("head", "blk", None), P("head", "blk", None),
            P("head"), P("head"), P("head", None), P(None, "head"), P("head"),
            P("head", None), P(None, "head"), P("head"),
            P("head"), P("head"), P("head"), P("head"), P("head"),
            P(None, "head", None), P(None, "head", None), P(), P(),
        ),
        out_specs=(P("blk", None, "head"), P("head", "blk", None), P("head", "blk", None)),
        check_vma=False,
    )
```

```python
import functools

import jax
import jax.numpy as jnp
from jax import lax
from jax.experimental import pallas as pl
from jax.experimental.pallas import tpu as pltpu
from jax.sharding import PartitionSpec as P

EPSILON = 1e-05
NORM_EPSILON = 0.00064
DECAY_SCALE = 0.6065306597126334

MESH = pl.DeviceIdType.MESH
F32 = jnp.float32
BF16 = jnp.bfloat16
I32 = jnp.int32

NB = 128
NH = 4
REQ = 8
STEPS = 16
WIDTH = 512
HEADS = 8
HW = 64
ROWS = 32
NI = 24
NC = 4
CROWS = ROWS // NC
CW = CROWS * HW
CT = CW // 128
CS = CT // 2
RB = 4

NT = (((1,), (1,)), ((), ()))
TN = (((0,), (0,)), ((), ()))
NN = (((1,), (0,)), ((), ()))


def mm(a, b, dims=NN):
    return lax.dot_general(a, b, dims, preferred_element_type=F32)


def hot(mask):
    return jnp.where(mask, 1.0, 0.0).astype(BF16)


def kernel(*refs):
    hbm, (tb_ref, back_r, back_er, put_ref) = refs[:NI], refs[NI : NI + 4]
    held, ss_i = refs[NI + 4 : 2 * NI + 4], refs[2 * NI + 4]
    loads = [pltpu.make_async_copy(hbm[i], held[i], ss_i.at[i]) for i in range(NI)]
    for i in (21, 19, 20, 22, 23, 4, 5, 3, 0, 1, 2) + tuple(range(6, 19)):
        loads[i].start()
    (
        x_ref, k_ref, v_ref, rq_ref, st_ref, ed_ref,
        ratio_d, ratio_r, off_d, off_r, erase, written, reward, gain, shift,
        left_d, right_d, left_r, right_r, dir_ref, tgt_ref, seqv_ref, seq_sm, app_sm,
    ) = held
    (
        stag, mid, recv, stag_e, mid_e, recv_e, back_s, back_m, back_es, back_em,
        r_recv, pb, pr, pb0, pr0,
        hi_s, tr_s, xs, kept, st_t,
        f_r, u_r, a_r, k_r, r_r, r_s, v_r, o_r, bonus_s,
        f_t, u_t, au_t, k_t, r_t, v_t, o_t,
        ss_e, rs_e, ss_h, rs_h,
    ) = refs[2 * NI + 5 :]
    me = lax.axis_index("blk")
    hd = lax.axis_index("head")
    z = lax.div(me, 16)
    y = lax.rem(lax.div(me, 2), 8)
    core = lax.rem(me, 2)
    z_off = [lax.rem(z + i, 8) * 16 for i in range(8)]
    y_off = [lax.rem(y + i, 8) * 2 for i in range(8)]
    c_off = [core, 1 - core]
    far = (4, 3, 5, 2, 6, 1, 7, 0)
    inner = [(b, c) for b in far for c in (1, 0)]

    barrier = pltpu.get_barrier_semaphore()
    for a in far[:-1]:
        pl.semaphore_signal(
            barrier, inc=1, device_id=(z_off[a] + lax.rem(me, 16), hd), device_id_type=MESH
        )
    for b, c in inner[:-1]:
        pl.semaphore_signal(
            barrier, inc=1, device_id=(z_off[0] + y_off[b] + c_off[c], hd), device_id_type=MESH
        )
    for i in range(1, NH):
        pl.semaphore_signal(barrier, inc=1, device_id=(me, lax.rem(hd + i, NH)), device_id_type=MESH)

    lane = lax.broadcasted_iota(I32, (NB, 128), 1)
    sub = lax.broadcasted_iota(I32, (NB, 128), 0)
    lane_f = lane.astype(F32)

    w = lax.rem(me, 16)

    def hop_z(src, dst, n):
        for a in far[:-1]:
            pltpu.make_async_remote_copy(
                src_ref=src.at[lax.rem(z + a, 8)], dst_ref=dst.at[z], send_sem=ss_e.at[n], recv_sem=rs_e.at[n],
                device_id=(z_off[a] + w, hd), device_id_type=MESH,
            ).start()
        dst[pl.ds(z, 1)] = src[pl.ds(z, 1)]

    def hop_w(src, dst, n):
        for b, c in inner[:-1]:
            to = y_off[b] + c_off[c]
            pltpu.make_async_remote_copy(
                src_ref=src.at[:, to], dst_ref=dst.at[:, w], send_sem=ss_e.at[n], recv_sem=rs_e.at[n],
                device_id=(z_off[0] + to, hd), device_id_type=MESH,
            ).start()
        dst[:, pl.ds(w, 1)] = src[:, pl.ds(w, 1)]

    def all_z(src, dst, n):
        return pltpu.make_async_remote_copy(
            src_ref=src.at[pl.ds(0, 7)], dst_ref=dst.at[pl.ds(0, 7)],
            send_sem=ss_e.at[n], recv_sem=rs_e.at[n], device_id=(me, hd), device_id_type=MESH,
        )

    def all_w(src, dst, n):
        return pltpu.make_async_remote_copy(
            src_ref=src.at[:, pl.ds(0, 15)], dst_ref=dst.at[:, pl.ds(0, 15)],
            send_sem=ss_e.at[n], recv_sem=rs_e.at[n], device_id=(me, hd), device_id_type=MESH,
        )

    for i in (21, 19, 20, 22, 23):
        loads[i].wait()

    fetch_q = jnp.zeros((2, 1024), I32)
    place_q = jnp.zeros((2, 1024), I32)
    for h in range(HEADS):
        dv = dir_ref[h]
        tv = tgt_ref[h]
        fetch_q = fetch_q + jnp.where((dv >> 7) == me, dv & 127, 0)
        place_q = place_q + jnp.where((tv >> 7) == me, tv & 127, 0)
        hi_s[2 * h : 2 * h + 2, :] = (dv >> 7).astype(F32)
        hi_s[16 + 2 * h : 18 + 2 * h, :] = (tv >> 7).astype(F32)
    both_q = jnp.sum((fetch_q + place_q * 128).astype(F32), axis=0, keepdims=True)
    seq_t = jnp.transpose(seqv_ref[...].astype(F32))
    cols = []
    for s in range(8):
        col = jnp.broadcast_to(seq_t[:, s : s + 1], (128, 128))
        acc = jnp.zeros((128, 128), F32)
        for qt in range(8):
            acc = acc + jnp.where(
                col == lane_f + float(128 * qt), both_q[:, qt * 128 : (qt + 1) * 128], 0.0
            )
        grouped = jnp.sum(acc.reshape(16, 8, 128), axis=1)
        cols.append(jnp.sum(grouped, axis=1, keepdims=True))
    both = jnp.concatenate(cols, axis=0)
    place = jnp.floor(both * (1.0 / 128.0))
    fetch = both - 128.0 * place
    pick = hot(fetch == lane_f)
    put_ref[...] = hot(place == lane_f)

    loads[5].wait()
    edges = jnp.concatenate([ed_ref[...], jnp.zeros((96, 128), F32)], axis=0).astype(BF16)
    stag_e[...] = mm(pick, edges, NT).reshape(8, 16, 1, 128)

    def lay(dst, src, ct):
        for c in range(ct):
            tr_s[pl.ds(c, NB, stride=ct), :] = src[:, c * 128 : (c + 1) * 128]
        dst[...] = tr_s[pl.ds(0, NB * ct), :].reshape(dst.shape).astype(BF16)

    def lay_piece(dst, src):
        for half in range(2):
            lay(dst.at[half], src[:, half * CS * 128 : (half + 1) * CS * 128], CS)

    def gather(cc):
        lay_piece(stag.at[cc], mm(pick, st_ref[:, cc * CW : (cc + 1) * CW].astype(BF16)))
        first_hop(stag, mid, cc, fetch_n)

    def first_hop(src, dst, cc, n):
        hop_z(src.at[cc, 0], dst.at[cc, 0], n + 4 * cc)
        hop_w(src.at[cc, 1], dst.at[cc, 1], n + 4 * cc + 1)

    def first_all(src, dst, cc, n):
        return (
            all_z(src.at[cc, 0], dst.at[cc, 0], n + 4 * cc),
            all_w(src.at[cc, 1], dst.at[cc, 1], n + 4 * cc + 1),
        )

    def second_hop(src, between, dst, cc, n):
        first_z, first_w = first_all(src, between, cc, n)
        first_z.wait_recv()
        hop_w(between.at[cc, 0], dst.at[cc, 0], n + 4 * cc + 2)
        first_w.wait_recv()
        hop_z(between.at[cc, 1], dst.at[cc, 1], n + 4 * cc + 3)

    def second_all(src, dst, cc, n):
        return (
            all_w(src.at[cc, 0], dst.at[cc, 0], n + 4 * cc + 2),
            all_z(src.at[cc, 1], dst.at[cc, 1], n + 4 * cc + 3),
        )

    def received(copies):
        for copy in copies:
            copy.wait_recv()

    def sent(copies):
        for copy in copies:
            copy.wait_send()

    fetch_n, back_n = 4, 4 + 4 * NC

    pl.semaphore_wait(barrier, 7 + 15 + NH - 1)
    hop_z(stag_e, mid_e, 0)
    loads[4].wait()
    gather(0)

    for i in (3, 0, 1, 2) + tuple(range(6, 19)):
        loads[i].wait()
    xf = x_ref[...].astype(F32)
    xs[:, 8:24, :] = xf
    xs[:, 0:8, :] = jnp.zeros((REQ, 8, WIDTH), F32)
    prev = xs[:, 7:23, :]

    def mix(cur, before, ratio):
        return (cur + (before - cur) * ratio).astype(BF16)

    delta_rows = (REQ * STEPS, WIDTH)
    md = mix(xf, prev, ratio_d[...].reshape(1, 1, WIDTH)).reshape(delta_rows)
    mr = mix(xf, prev, ratio_r[...].reshape(1, 1, WIDTH)).reshape(delta_rows)
    pb[0] = mm(left_d[...], md, NT).astype(BF16)
    pb[1] = mm(left_r[...], mr, NT).astype(BF16)
    def to_heads(src, dst, n):
        for i in range(1, NH):
            pltpu.make_async_remote_copy(
                src_ref=src(lax.rem(hd + i, NH)), dst_ref=dst.at[hd], send_sem=ss_h.at[n], recv_sem=rs_h.at[n],
                device_id=(me, lax.rem(hd + i, NH)), device_id_type=MESH,
            ).start()

    def heads_of(dst, n):
        return pltpu.make_async_remote_copy(
            src_ref=dst.at[pl.ds(0, NH - 1)], dst_ref=dst.at[pl.ds(0, NH - 1)],
            send_sem=ss_h.at[n], recv_sem=rs_h.at[n], device_id=(me, hd), device_id_type=MESH,
        )

    def part(g):
        return rq_ref.at[:, :, pl.ds(pl.multiple_of(g * WIDTH, WIDTH), WIDTH)]

    to_heads(lambda g: pb, pr, 1)
    to_heads(part, r_recv, 0)
    all_z(stag_e, mid_e, 0).wait_recv()
    hop_w(mid_e, recv_e, 1)
    for cc in range(1, NC):
        gather(cc)

    row8 = lax.broadcasted_iota(I32, (REQ, 1024), 0)
    lane1024 = lax.broadcasted_iota(I32, (REQ, 1024), 1)
    q_of = jnp.zeros((REQ, 1024), I32)
    count_row = jnp.zeros((1, 128), I32)
    count_col = jnp.zeros((REQ, WIDTH), I32)
    lane1 = lax.broadcasted_iota(I32, (1, 128), 1)
    row8w = lax.broadcasted_iota(I32, (REQ, WIDTH), 0)
    for i in range(REQ):
        q = seq_sm[me * REQ + i]
        n = app_sm[q]
        q_of = jnp.where(row8 == i, q, q_of)
        count_row = jnp.where(lax.rem(lane1, 8) == i, n, count_row)
        count_col = jnp.where(row8w == i, n, count_col)
    own = jnp.where(q_of == lane1024, 1.0, 0.0)
    own = jnp.concatenate([own] * 16, axis=0).astype(BF16)
    spread = mm(hi_s[...].astype(BF16), own, NT)
    r_id = lax.broadcasted_iota(I32, (16, 128), 0)
    l_id = lax.broadcasted_iota(I32, (16, 128), 1)
    group = lax.rem(r_id, 2) * 8 + lax.rem(lax.div(r_id, 2), 2) * 4 + lax.div(r_id, 4)
    mine = lax.div(l_id, 8) == group
    holder = jnp.sum(jnp.where(mine, spread[:16], 0.0), axis=0, keepdims=True)
    owner = jnp.sum(jnp.where(mine, spread[16:], 0.0), axis=0, keepdims=True)
    sub_f = sub.astype(F32)
    from_holder = hot(sub_f == holder)
    to_owner = hot(sub_f == owner)

    pr[pl.ds(hd, 1)] = pb[...].reshape(1, 2, 96, 128)
    r_recv[pl.ds(hd, 1)] = rq_ref[:, :, pl.ds(pl.multiple_of(hd * WIDTH, WIDTH), WIDTH)].reshape(
        1, REQ, 4, WIDTH
    )
    heads_of(r_recv, 0).wait_recv()
    for g in range(NH):
        r_r[:, 4 * g : 4 * g + 4, :] = r_recv[g].astype(F32)

    def put_rows(ref, val):
        for p in range(4):
            ref[p] = val[:, p * 128 : (p + 1) * 128]

    def get_rows(ref):
        return jnp.concatenate([ref[p] for p in range(4)], axis=1)

    def put_step(ref, t, val):
        for p in range(4):
            ref[p, pl.ds(t, REQ, stride=STEPS), :] = val[:, p * 128 : (p + 1) * 128]

    def second(summed_d, summed_r, dims):
        hidden = jnp.tanh(summed_d).astype(BF16)
        zz = off_d[...] + mm(hidden, right_d[...], dims)
        keep = jnp.exp(-DECAY_SCALE * jax.nn.sigmoid(zz))
        rate = jax.nn.sigmoid(off_r[...] + mm(summed_r.astype(BF16), right_r[...], dims))
        return keep, rate

    kf = k_ref[...].astype(F32).reshape(delta_rows)
    put_rows(u_r, kf * erase[...])
    put_rows(v_r, v_ref[...].astype(F32).reshape(delta_rows))
    put_rows(r_s, r_r[...].reshape(delta_rows))

    heads_of(pr, 1).wait_recv()
    sums = pr[0].astype(F32) + pr[1].astype(F32) + pr[2].astype(F32) + pr[3].astype(F32)
    keep, rate = second(sums[0], sums[1], TN)
    put_rows(f_r, keep)
    put_rows(a_r, rate)
    put_rows(k_r, kf * (1.0 + (rate - 1.0) * written[...]))

    def turn(ref, tp):
        first = [ref[p, pl.ds(2 * tp, REQ, stride=STEPS), :] for p in range(4)]
        other = [ref[p, pl.ds(2 * tp + 1, REQ, stride=STEPS), :] for p in range(4)]
        rows = []
        for at in (0, 64):
            for p in range(4):
                rows.append(jnp.concatenate([first[p][:, at : at + 64], other[p][:, at : at + 64]], axis=1))
        return jnp.transpose(jnp.concatenate(rows + rows, axis=0))

    def turn_pair(tp, carry):
        def put_pair(dst, val):
            dst[pl.ds(2 * tp, 2)] = val.reshape(2, HW, 128)

        put_pair(f_t, turn(f_r, tp))
        put_pair(k_t, turn(k_r, tp))
        put_pair(r_t, turn(r_s, tp))
        u = turn(u_r, tp).reshape(2, HW, 128)
        u = u * lax.rsqrt(jnp.sum(u * u, axis=1, keepdims=True) + EPSILON)
        u_t[pl.ds(2 * tp, 2)] = u
        au_t[pl.ds(2 * tp, 2)] = turn(a_r, tp).reshape(2, HW, 128) * u
        return carry

    def turn_values(tq, carry):
        steps = [[v_r[p, pl.ds(4 * tq + i, REQ, stride=STEPS), :] for p in range(4)] for i in range(4)]
        rows = []
        for half in range(2):
            for odd in range(2):
                for p in range(4):
                    at = odd * 64 + half * 32
                    rows.append(jnp.concatenate([s[p][:, at : at + 32] for s in steps], axis=1))
        v_t[pl.ds(4 * tq, 4)] = jnp.transpose(jnp.concatenate(rows, axis=0)).reshape(4, ROWS, 128)
        return carry

    lax.fori_loop(0, 4, turn_values, 0)

    lax.fori_loop(1, 8, turn_pair, 0)

    def pass_on(cc):
        second_hop(stag, mid, recv, cc, fetch_n)

    pass_on(0)

    all_w(mid_e, recv_e, 1).wait_recv()
    by_item = mm(from_holder, recv_e[...].reshape(NB, 128).astype(BF16), TN)
    edge_cols = []
    for p in range(4):
        parts = []
        for odd in range(2):
            for half in range(2):
                at = half * 64 + odd * 32 + p * 8
                parts.append(by_item[at : at + 8, 0:32])
        edge_cols.append(jnp.concatenate(parts, axis=1))
    edge = jnp.concatenate(edge_cols, axis=1)
    x0 = xs[:, 8, :]
    pb0[...] = jnp.zeros(pb0.shape, F32)
    pb0[0, :, 0:96] = mm(mix(x0, edge, ratio_d[...]), left_d[...], NT)
    pb0[1, :, 0:96] = mm(mix(x0, edge, ratio_r[...]), left_r[...], NT)
    to_heads(lambda g: pb0, pr0, 2)
    pass_on(1)
    pr0[pl.ds(hd, 1)] = pb0[...].reshape(1, 2, REQ, 128)


    new_edge = jnp.where(count_col == 0, edge, 0.0)
    for t in range(STEPS):
        new_edge = new_edge + jnp.where(count_col == t + 1, xs[:, 8 + t, :], 0.0)
    items = []
    for half in range(2):
        for odd in range(2):
            for p in range(4):
                at = p * 128 + odd * 64 + half * 32
                items.append(new_edge[:, at : at + 32])
    items = jnp.concatenate(items, axis=0)
    items = jnp.concatenate([items, jnp.zeros((NB, 96), F32)], axis=1)
    back_es[...] = mm(to_owner, items.astype(BF16)).reshape(8, 16, 1, 128)
    hop_z(back_es, back_em, 2)

    heads_of(pr0, 2).wait_recv()
    sums0 = (pr0[0] + pr0[1] + pr0[2] + pr0[3])[:, :, :96]
    keep0, rate0 = second(sums0[0], sums0[1], NN)
    k0 = k_ref[...].astype(F32)[:, 0, :]
    put_step(f_r, 0, keep0)
    put_step(a_r, 0, rate0)
    put_step(k_r, 0, k0 * (1.0 + (rate0 - 1.0) * written[...]))
    turn_pair(0, 0)
    pass_on(2)

    def advance_rows(row0, local0):
        start = [st_t[pl.ds(pl.multiple_of((local0 + i) * HW, HW), HW), :] for i in range(RB)]
        for i in range(RB):
            kept[pl.ds(pl.multiple_of((local0 + i) * HW, HW), HW), :] = start[i]

        def step(t, states):
            u, f, au, kk, r = u_t[t], f_t[t], au_t[t], k_t[t], r_t[t]
            taken = jnp.broadcast_to(count_row == t + 1, (HW, 128))
            out = []
            for i in range(RB):
                s = states[i]
                v = v_t[t, pl.ds(row0 + i, 1), :]
                proj = jnp.sum(s * u, axis=0, keepdims=True)
                s = s * f - proj * au + v * kk
                o_t[t, pl.ds(row0 + i, 1), :] = jnp.sum(s * r, axis=0, keepdims=True)
                where = pl.ds(pl.multiple_of((local0 + i) * HW, HW), HW)
                kept[where, :] = jnp.where(taken, s, kept[where, :])
                out.append(s)
            return tuple(out)

        lax.fori_loop(0, STEPS, step, tuple(start), unroll=4)

    def return_on(cc):
        second_hop(back_s, back_m, back_r, cc, back_n)

    for cc in range(NC):
        received(second_all(mid, recv, cc, fetch_n))
        for half in range(2):
            tr_s[half * NB * CS : (half + 1) * NB * CS, :] = recv[cc, half].astype(F32).reshape(NB * CS, 128)
        for c in range(CT):
            block = tr_s[pl.ds(c // CS * NB * CS + c % CS, NB, stride=CS), :].astype(BF16)
            st_t[c * 128 : (c + 1) * 128, :] = mm(block, from_holder, TN)

        def rows(ib, carry, cc=cc):
            advance_rows(cc * CROWS + ib * RB, ib * RB)
            return carry

        lax.fori_loop(0, CROWS // RB, rows, 0)
        lay_piece(back_s.at[cc], mm(to_owner, kept[...].astype(BF16), NT))
        first_hop(back_s, back_m, cc, back_n)
        if cc == 0:
            pass_on(3)
            all_z(back_es, back_em, 2).wait_recv()
            hop_w(back_em, back_er, 3)
        if cc >= 2:
            return_on(cc - 2)

    product = get_rows(r_s) * get_rows(k_r) * reward[...]
    high = product.astype(BF16)
    low = (product - high.astype(F32)).astype(BF16)
    b_row = lax.broadcasted_iota(I32, (WIDTH, WIDTH), 0)
    b_col = lax.broadcasted_iota(I32, (WIDTH, WIDTH), 1)
    same = hot(lax.div(b_row, HW) == lax.div(b_col, HW))
    bonus_s[...] = (mm(high, same) + mm(low, same)) * get_rows(v_r)

    return_on(NC - 2)

    def finish(tq, carry):
        o = o_t[pl.ds(4 * tq, 4)]
        total = jnp.sum(o, axis=1)
        mean = (total + pltpu.roll(total, 64, 1)) * (1.0 / HW)
        cen = o - mean.reshape(4, 1, 128)
        square = jnp.sum(cen * cen, axis=1)
        var = (square + pltpu.roll(square, 64, 1)) * (1.0 / HW)
        norm = cen * lax.rsqrt(var + NORM_EPSILON).reshape(4, 1, 128)
        flat = jnp.transpose(norm.reshape(128, 128))
        for i in range(4):
            pieces = []
            for p in range(4):
                for odd in range(2):
                    for half in range(2):
                        at = half * 64 + odd * 32 + p * 8
                        pieces.append(flat[at : at + 8, i * 32 : (i + 1) * 32])
            put_step(o_r, 4 * tq + i, jnp.concatenate(pieces, axis=1))
        return carry

    lax.fori_loop(0, 4, finish, 0)
    return_on(NC - 1)
    result = get_rows(o_r) * gain[...] + shift[...] + bonus_s[...]
    tb_ref[...] = result.astype(BF16).reshape(REQ, STEPS, WIDTH)

    all_w(back_em, back_er, 3).wait_recv()
    for cc in range(NC):
        received(second_all(back_m, back_r, cc, back_n))
    all_z(stag_e, mid_e, 0).wait_send()
    all_w(mid_e, recv_e, 1).wait_send()
    all_z(back_es, back_em, 2).wait_send()
    all_w(back_em, back_er, 3).wait_send()
    for cc in range(NC):
        sent(first_all(stag, mid, cc, fetch_n))
        sent(second_all(mid, recv, cc, fetch_n))
        sent(first_all(back_s, back_m, cc, back_n))
        sent(second_all(back_m, back_r, cc, back_n))
    heads_of(r_recv, 0).wait_send()
    heads_of(pr, 1).wait_send()
    heads_of(pr0, 2).wait_send()


def settle(tb_ref, back_r, back_er, put_ref, out_ref, ns_ref, ne_ref, tr_s):
    out_ref[...] = tb_ref[...]
    put = put_ref[...]
    ne_ref[...] = mm(back_er[...].reshape(NB, 128).astype(BF16), put, TN)[0:32]
    put_t = jnp.transpose(put.astype(F32)).astype(BF16)
    for cc in range(NC):
        for half in range(2):
            tr_s[half * NB * CS : (half + 1) * NB * CS, :] = back_r[cc, half].astype(F32).reshape(NB * CS, 128)
        for c in range(CT):
            block = tr_s[pl.ds(c // CS * NB * CS + c % CS, NB, stride=CS), :].astype(BF16)
            at = cc * CW + c * 128
            ns_ref[:, at : at + 128] = mm(put_t, block)


def local(
    layer_entry_vectors, guessed_lookup_vectors, guessed_content_vectors, gating_query,
    lane_memory_store, prior_step_store, fading_blend_ratio, learning_speed_blend,
    fading_left_factor, fading_right_factor, fading_offset,
    learning_speed_left, learning_speed_right, learning_speed_offset,
    erasing_lookup_factor, written_lookup_factor, present_reward_factors,
    lane_standard_factor, lane_standard_offset,
    caller_memory_directory, kept_target_place, caller_sequence, approved_guesses,
):
    def row(vector):
        return vector.reshape(1, WIDTH)

    vmem = pl.BlockSpec(memory_space=pltpu.VMEM)
    dma = pltpu.SemaphoreType.DMA
    rows = REQ * STEPS
    arrays = (
        layer_entry_vectors, guessed_lookup_vectors, guessed_content_vectors, gating_query,
        lane_memory_store.reshape(NB, 2048), jnp.transpose(prior_step_store[0]),
        row(fading_blend_ratio), row(learning_speed_blend), row(fading_offset), row(learning_speed_offset),
        row(erasing_lookup_factor), row(written_lookup_factor), row(present_reward_factors),
        row(lane_standard_factor), row(lane_standard_offset),
        jnp.transpose(fading_left_factor), fading_right_factor,
        jnp.transpose(learning_speed_left), learning_speed_right,
        jnp.transpose(caller_memory_directory, (1, 2, 0)), jnp.transpose(kept_target_place, (1, 2, 0)),
        caller_sequence.reshape(8, 128), caller_sequence, approved_guesses,
    )
    hbm = pl.BlockSpec(memory_space=pltpu.HBM)
    outs = pl.pallas_call(
        kernel,
        out_shape=(
            jax.ShapeDtypeStruct((REQ, STEPS, WIDTH), BF16),
            jax.ShapeDtypeStruct((NC, 2, 8, 16, CS, 128), BF16),
            jax.ShapeDtypeStruct((8, 16, 1, 128), F32),
            jax.ShapeDtypeStruct((NB, 128), BF16),
        ),
        in_specs=[hbm] * NI,
        out_specs=(vmem,) * 4,
        scratch_shapes=[pltpu.VMEM(a.shape, a.dtype) for a in arrays[:-2]]
        + [pltpu.SMEM(a.shape, a.dtype) for a in arrays[-2:]]
        + [
            dma((NI,)),
            pltpu.VMEM((NC, 2, 8, 16, CS, 128), BF16),
            pltpu.VMEM((NC, 2, 8, 16, CS, 128), BF16),
            pltpu.VMEM((NC, 2, 8, 16, CS, 128), BF16),
            pltpu.VMEM((8, 16, 1, 128), F32),
            pltpu.VMEM((8, 16, 1, 128), F32),
            pltpu.VMEM((8, 16, 1, 128), F32),
            pltpu.VMEM((NC, 2, 8, 16, CS, 128), BF16),
            pltpu.VMEM((NC, 2, 8, 16, CS, 128), BF16),
            pltpu.VMEM((8, 16, 1, 128), F32),
            pltpu.VMEM((8, 16, 1, 128), F32),
            pltpu.VMEM((NH, REQ, 4, WIDTH), BF16),
            pltpu.VMEM((2, 96, 128), BF16),
            pltpu.VMEM((NH, 2, 96, 128), BF16),
            pltpu.VMEM((2, REQ, 128), F32),
            pltpu.VMEM((NH, 2, REQ, 128), F32),
            pltpu.VMEM((32, 1024), F32),
            pltpu.VMEM((NB * CT, 128), F32),
            pltpu.VMEM((REQ, 24, WIDTH), F32),
            pltpu.VMEM((CW, 128), F32),
            pltpu.VMEM((CW, 128), F32),
            pltpu.VMEM((4, rows, 128), F32),
            pltpu.VMEM((4, rows, 128), F32),
            pltpu.VMEM((4, rows, 128), F32),
            pltpu.VMEM((4, rows, 128), F32),
            pltpu.VMEM((REQ, STEPS, WIDTH), F32),
            pltpu.VMEM((4, rows, 128), F32),
            pltpu.VMEM((4, rows, 128), F32),
            pltpu.VMEM((4, rows, 128), F32),
            pltpu.VMEM((rows, WIDTH), F32),
            pltpu.VMEM((STEPS, HW, 128), F32),
            pltpu.VMEM((STEPS, HW, 128), F32),
            pltpu.VMEM((STEPS, HW, 128), F32),
            pltpu.VMEM((STEPS, HW, 128), F32),
            pltpu.VMEM((STEPS, HW, 128), F32),
            pltpu.VMEM((STEPS, ROWS, 128), F32),
            pltpu.VMEM((STEPS, ROWS, 128), F32),
            dma((4 + 8 * NC,)), dma((4 + 8 * NC,)), dma((3,)), dma((3,)),
        ],
        compiler_params=pltpu.CompilerParams(
            collective_id=0, has_side_effects=True, vmem_limit_bytes=24 << 20
        ),
        name="draft_check",
    )(
        *[pltpu.with_memory_space_constraint(a, pltpu.HBM) for a in arrays]
    )
    result, states, edges = pl.pallas_call(
        settle,
        out_shape=(
            jax.ShapeDtypeStruct((REQ, STEPS, WIDTH), BF16),
            jax.ShapeDtypeStruct((NB, 2048), F32),
            jax.ShapeDtypeStruct((32, NB), F32),
        ),
        in_specs=[vmem] * 4,
        out_specs=(vmem,) * 3,
        scratch_shapes=[pltpu.VMEM((NB * CT, 128), F32)],
        compiler_params=pltpu.CompilerParams(vmem_limit_bytes=12 << 20),
        name="settle",
    )(*outs)
    return (result, states[None], jnp.transpose(edges)[None])


def solution(mesh):
    return jax.shard_map(
        local,
        mesh=mesh,
        in_specs=(
            P("blk", None, "head"), P("blk", None, "head"), P("blk", None, "head"), P("blk", "head", None),
            P("head", "blk", None), P("head", "blk", None),
            P("head"), P("head"), P("head", None), P(None, "head"), P("head"),
            P("head", None), P(None, "head"), P("head"),
            P("head"), P("head"), P("head"), P("head"), P("head"),
            P(None, "head", None), P(None, "head", None), P(), P(),
        ),
        out_specs=(P("blk", None, "head"), P("head", "blk", None), P("head", "blk", None)),
        check_vma=False,
    )
```
